512 devices in a mesh: dp: 16 (over z, core), mp: 32 (over y, x).
Axes of the slice: x: 4, y: 8, z: 8, core: 2. Of those that a mesh axis runs over, the one named last changes fastest.
Arguments:
- policy_hidden: bfloat16 [1024, 3584], P('dp'), may hold values from -96 to 96
- reference_hidden: bfloat16 [1024, 3584], P('dp'), may hold values from -96 to 96
- policy_gain: float32 [3584], replicated, may hold values from 0.5 to 1.5
- reference_gain: float32 [3584], replicated, may hold values from 0.5 to 1.5
- policy_embedding: bfloat16 [131072, 3584], P(('dp', 'mp')), may hold values from -1 to 1
- reference_embedding: bfloat16 [131072, 3584], P(('dp', 'mp')), may hold values from -1 to 1
- mixture_weight: float32 [1024], replicated, may hold values from 0.1 to 0.9
- sampled_tokens: int32 [1024], replicated, may hold values from 0 to 131071
Outputs:
- mixture_shift: float32 [1024, 131072], P(None, ('dp', 'mp'))
- sampled_logprobs: float32 [3, 1024], P(None, 'dp')
The draws below stay inside these ranges and needn't reach their ends.
All inputs are finite; a program needn't handle non-finite values.
Results may differ from the reference program's by a relative error of at most 0.002.
Values may be sent and summed in bfloat16 or wider, within the bound.
No kernel may reach another device: no remote copies, remote signals or barrier semaphores. Data moves between devices by JAX's collectives and lax.ppermute only.
A program may use at most 64 MiB of HBM per device.

```python
import math
import jax
import jax.numpy as jnp
from jax import lax

D = 3584
VOCAB = 131072
BATCH = 1024


def hidden_states(key):
    keys = jax.random.split(key, 3)
    rows = jnp.exp(jax.random.uniform(keys[1], (BATCH, 1), jnp.float32, 0.0, math.log(10.0)))
    columns = jnp.exp(jax.random.uniform(keys[2], (1, D), jnp.float32, -1.15, 1.15))
    base = jax.random.normal(keys[0], (BATCH, D), jnp.float32)
    return jnp.clip(base * rows * columns, -96.0, 96.0).astype(jnp.bfloat16)


def embedding_rows(key):
    keys = jax.random.split(key, 2)
    place = jnp.arange(VOCAB, dtype=jnp.float32)[:, None] / VOCAB
    jitter = jnp.exp(jax.random.uniform(keys[1], (VOCAB, 1), jnp.float32, -0.5, 0.5))
    scale = 4.0 / math.sqrt(D) * (0.6 + 1.2 * place) * jitter
    base = jax.random.normal(keys[0], (VOCAB, D), jnp.float32)
    return jnp.clip(base * scale, -1.0, 1.0).astype(jnp.bfloat16)


def draw_policy_hidden(key, part):
    return hidden_states(jax.random.fold_in(key, 11))


def draw_reference_hidden(key, part):
    return hidden_states(jax.random.fold_in(key, 12))


def draw_policy_embedding(key, part):
    return embedding_rows(jax.random.fold_in(key, 21))


def draw_reference_embedding(key, part):
    return embedding_rows(jax.random.fold_in(key, 22))


def plant(array, own_key, least, high):
    extent = array.shape
    index_at = [jax.random.randint(jax.random.fold_in(own_key, axis), (), 0, extent[axis]) for axis in range(len(extent))]
    array = array.at[tuple(index_at)].set(least)
    longest = extent.index(max(extent))
    index_at[longest] = (index_at[longest] + 1) % extent[longest]
    return array.at[tuple(index_at)].set(high)


def setup_inputs(seed: int = 0) -> dict:
    key_of = jax.random.split(jax.random.key(seed), 9)
    return {
        "policy_hidden": draw_policy_hidden(jax.random.fold_in(key_of[8], 71), 0),
        "reference_hidden": draw_reference_hidden(jax.random.fold_in(key_of[8], 71), 0),
        "policy_gain": jnp.clip(1.0 + 0.1 * jax.random.normal(key_of[2], (D,), jnp.float32), 0.5, 1.5),
        "reference_gain": jnp.clip(1.0 + 0.1 * jax.random.normal(key_of[3], (D,), jnp.float32), 0.5, 1.5),
        "policy_embedding": draw_policy_embedding(jax.random.fold_in(key_of[8], 71), 0),
        "reference_embedding": draw_reference_embedding(jax.random.fold_in(key_of[8], 71), 0),
        "mixture_weight": jnp.clip(jax.random.uniform(key_of[6], (BATCH,), jnp.float32, 0.1, 0.9), 0.1, 0.9),
        "sampled_tokens": plant(jax.random.randint(key_of[7], (BATCH,), 0, VOCAB), jax.random.fold_in(key_of[7], 1), 0, VOCAB - 1).astype(jnp.int32),
    }


softcap = 30.0
epsilon = 1e-06

def normalize(hidden, gain):
    values = hidden.astype(jnp.float32)
    meansq = lax.optimization_barrier(jnp.mean(values * values, axis=-1, keepdims=True))
    return (values * lax.rsqrt(meansq + epsilon) * gain).astype(jnp.bfloat16)

def project(normed, embedding):
    raw = lax.dot_general(normed, embedding, (((1,), (1,)), ((), ())), preferred_element_type=jnp.float32)
    return softcap * jnp.tanh(raw / softcap)

def reference(policy_hidden, reference_hidden, policy_gain, reference_gain, policy_embedding, reference_embedding, mixture_weight, sampled_tokens):
    capped_policy = project(normalize(policy_hidden, policy_gain), policy_embedding)
    capped_reference = project(normalize(reference_hidden, reference_gain), reference_embedding)
    weight = mixture_weight[:, None]
    mixed = (1.0 - weight) * capped_policy + weight * capped_reference
    policy_total = jnp.log(lax.optimization_barrier(jnp.sum(jnp.exp(capped_policy), axis=1)))
    reference_total = jnp.log(lax.optimization_barrier(jnp.sum(jnp.exp(capped_reference), axis=1)))
    mixture_total = jnp.log(lax.optimization_barrier(jnp.sum(jnp.exp(mixed), axis=1)))
    mixture_shift = mixed - mixture_total[:, None] - (capped_policy - policy_total[:, None])
    chosen = sampled_tokens.astype(jnp.int32)[:, None]
    policy_pick = jnp.take_along_axis(capped_policy, chosen, axis=1)[:, 0]
    reference_pick = jnp.take_along_axis(capped_reference, chosen, axis=1)[:, 0]
    mixed_pick = (1.0 - mixture_weight) * policy_pick + mixture_weight * reference_pick
    sampled_logprobs = jnp.stack([policy_pick - policy_total, reference_pick - reference_total, mixed_pick - mixture_total])
    return (mixture_shift, sampled_logprobs)
```

```python
import jax
import jax.numpy as jnp
from jax import lax
from jax.experimental import pallas as pl
from jax.experimental.pallas import tpu as pltpu
from jax.sharding import Mesh
from jax.sharding import PartitionSpec as P

DP = ("dp_0", "dp_1")
MP = ("mp_0", "mp_1")
DP_MP = ("dp_0", "dp_1", "mp_0", "mp_1")

softcap = 30.0
epsilon = 1e-06

VMEM_LIMIT = 48 * 1024 * 1024


def normalize_kernel(half_ref, policy_ref, reference_ref, policy_gain_ref, reference_gain_ref, out_ref):
    for model, (hidden_ref, gain_ref) in enumerate(
        ((policy_ref, policy_gain_ref), (reference_ref, reference_gain_ref))
    ):
        values = hidden_ref[...].astype(jnp.float32)
        meansq = jnp.mean(values * values, axis=-1, keepdims=True)
        normed = values * lax.rsqrt(meansq + epsilon) * gain_ref[...]
        out_ref[model] = normed.astype(jnp.bfloat16)


def normalize(half, policy_hidden, reference_hidden, policy_gain, reference_gain):
    rows, width = policy_hidden.shape
    part = rows // 2
    hidden_spec = pl.BlockSpec((part, width), lambda i, half: (half[0], 0))
    gain_spec = pl.BlockSpec((1, width), lambda i, half: (0, 0))
    return pl.pallas_call(
        normalize_kernel,
        grid_spec=pltpu.PrefetchScalarGridSpec(
            num_scalar_prefetch=1,
            grid=(1,),
            in_specs=[hidden_spec, hidden_spec, gain_spec, gain_spec],
            out_specs=pl.BlockSpec((2, part, width), lambda i, half: (0, 0, 0)),
        ),
        out_shape=jax.ShapeDtypeStruct((2, part, width), jnp.bfloat16),
        compiler_params=pltpu.CompilerParams(vmem_limit_bytes=VMEM_LIMIT),
        name="normalize",
    )(half, policy_hidden, reference_hidden, policy_gain, reference_gain)


def mixture_kernel(
    hidden_ref,
    policy_own_ref,
    policy_other_ref,
    reference_own_ref,
    reference_other_ref,
    weight_ref,
    token_ref,
    diff_own_ref,
    diff_other_ref,
    sums_ref,
    policy_acc,
    reference_acc,
):
    step = pl.program_id(0)
    shards, _, part, depth = hidden_ref.shape
    vocab = policy_own_ref.shape[0]
    seqs = shards * part

    @pl.when(step == 0)
    def _():
        policy_acc[...] = jnp.zeros_like(policy_acc)
        reference_acc[...] = jnp.zeros_like(reference_acc)

    for model, (own_ref, other_ref, acc) in enumerate(
        (
            (policy_own_ref, policy_other_ref, policy_acc),
            (reference_own_ref, reference_other_ref, reference_acc),
        )
    ):
        hidden = hidden_ref[:, model].reshape(seqs, depth)
        for place, rows_ref in enumerate((own_ref, other_ref)):
            acc[pl.ds(place * vocab, vocab), :] += lax.dot_general(
                rows_ref[...], hidden, (((1,), (1,)), ((), ())), preferred_element_type=jnp.float32
            )

    @pl.when(step == pl.num_programs(0) - 1)
    def _():
        weight = weight_ref[...]
        keep = 1.0 - weight
        totals = [jnp.zeros((8, seqs), jnp.float32) for _ in range(5)]
        for place, diff_ref in enumerate((diff_own_ref, diff_other_ref)):
            token = token_ref[place : place + 1, :]

            def body(i, carry, place=place, diff_ref=diff_ref, token=token):
                row = pl.multiple_of(i * 8, 8)
                policy = softcap * jnp.tanh(policy_acc[pl.ds(place * vocab + row, 8), :] * (1.0 / softcap))
                reference = softcap * jnp.tanh(
                    reference_acc[pl.ds(place * vocab + row, 8), :] * (1.0 / softcap)
                )
                mixed = keep * policy + weight * reference
                diff_ref[pl.ds(row, 8), :] = mixed - policy
                hit = lax.broadcasted_iota(jnp.int32, (8, seqs), 0) + row == token
                return (
                    carry[0] + jnp.exp(policy),
                    carry[1] + jnp.exp(mixed),
                    carry[2] + jnp.exp(reference),
                    carry[3] + jnp.where(hit, policy, 0.0),
                    carry[4] + jnp.where(hit, reference, 0.0),
                )

            totals = lax.fori_loop(0, vocab // 8, body, tuple(totals))
        for k in range(5):
            sums_ref[k : k + 1, :] = jnp.sum(totals[k], axis=0, keepdims=True)


def mixture(hidden, policy_own, policy_other, reference_own, reference_other, weight, token):
    shards, _, part, width = hidden.shape
    vocab = policy_own.shape[0]
    seqs = shards * part
    depth = width // 7
    rows_spec = pl.BlockSpec((vocab, depth), lambda k: (0, k))
    whole = lambda *shape: pl.BlockSpec(shape, lambda k: (0,) * len(shape))
    return pl.pallas_call(
        mixture_kernel,
        grid=(width // depth,),
        in_specs=[
            pl.BlockSpec((shards, 2, part, depth), lambda k: (0, 0, 0, k)),
            rows_spec,
            rows_spec,
            rows_spec,
            rows_spec,
            whole(1, seqs),
            whole(2, seqs),
        ],
        out_specs=[whole(vocab, seqs), whole(vocab, seqs), whole(5, seqs)],
        out_shape=[
            jax.ShapeDtypeStruct((vocab, seqs), jnp.float32),
            jax.ShapeDtypeStruct((vocab, seqs), jnp.float32),
            jax.ShapeDtypeStruct((5, seqs), jnp.float32),
        ],
        scratch_shapes=[
            pltpu.VMEM((2 * vocab, seqs), jnp.float32),
            pltpu.VMEM((2 * vocab, seqs), jnp.float32),
        ],
        compiler_params=pltpu.CompilerParams(vmem_limit_bytes=VMEM_LIMIT),
        name="mixture",
    )(hidden, policy_own, policy_other, reference_own, reference_other, weight, token)


def shift_kernel(half_ref, own_ref, other_ref, delta_ref, out_ref):
    block = out_ref.shape
    for turn, diff_ref in enumerate((own_ref, other_ref)):

        @pl.when(pl.program_id(0) == turn)
        def _(turn=turn, diff_ref=diff_ref):
            shifted = diff_ref[...] + delta_ref[turn : turn + 1, :]
            out_ref[...] = shifted.T.reshape(block)


def shift(half, diff_own, diff_other, delta, shards):
    vocab, seqs = diff_own.shape
    part = seqs // shards
    chunk = 128
    per = chunk // part
    return pl.pallas_call(
        shift_kernel,
        grid_spec=pltpu.PrefetchScalarGridSpec(
            num_scalar_prefetch=1,
            grid=(2, seqs // chunk),
            in_specs=[
                pl.BlockSpec((vocab, chunk), lambda t, j, half: (0, jnp.where(t == 0, j, seqs // chunk - 1))),
                pl.BlockSpec((vocab, chunk), lambda t, j, half: (0, jnp.where(t == 0, 0, j))),
                pl.BlockSpec((2, chunk), lambda t, j, half: (0, j)),
            ],
            out_specs=pl.BlockSpec((per, 1, part, vocab), lambda t, j, half: (j, half[0] ^ t, 0, 0)),
        ),
        out_shape=jax.ShapeDtypeStruct((shards, 2, part, vocab), jnp.float32),
        compiler_params=pltpu.CompilerParams(vmem_limit_bytes=VMEM_LIMIT),
        name="shift",
    )(half, diff_own, diff_other, delta)


def partners(z, y, x):
    pairs = []
    for source in range(z * 2 * y * x):
        i, rest = divmod(source, 2 * y * x)
        c, rest = divmod(rest, y * x)
        j, k = divmod(rest, x)
        j, k = (j, k ^ 1) if c == 0 else (j ^ 1, k)
        pairs.append((source, ((i * 2 + c) * y + j) * x + k))
    return pairs


def everywhere(block, axes):
    group = lax.axis_size(axes)
    return lax.all_to_all(
        jnp.broadcast_to(block[None], (group,) + block.shape), axes, 0, 0, tiled=True
    )


def local(
    policy_hidden,
    reference_hidden,
    policy_gain,
    reference_gain,
    policy_embedding,
    reference_embedding,
    mixture_weight,
    sampled_tokens,
):
    seq_local = policy_hidden.shape[0]
    part = seq_local // 2
    vocab = policy_embedding.shape[0]
    shards = lax.axis_size(DP)
    copies = lax.axis_size(MP)
    shard = lax.axis_index(DP)
    copy = lax.axis_index(MP)
    core = lax.axis_index("dp_1")
    row = lax.axis_index("mp_0")
    column = lax.axis_index("mp_1")
    half = (row + column) % 2
    other_copy = jnp.where(
        core == 0,
        row * lax.axis_size("mp_1") + (column ^ 1),
        (row ^ 1) * lax.axis_size("mp_1") + column,
    )
    first_own = (shard * copies + copy) * vocab
    first_other = (shard * copies + other_copy) * vocab
    half_arg = half.astype(jnp.int32)[None]
    pairs = partners(lax.axis_size("dp_0"), lax.axis_size("mp_0"), lax.axis_size("mp_1"))

    normed = normalize(
        half_arg, policy_hidden, reference_hidden, policy_gain[None], reference_gain[None]
    )
    normed, policy_send, reference_send = lax.optimization_barrier(
        (normed, policy_embedding, reference_embedding)
    )
    hidden = lax.all_gather(normed, DP, axis=0)
    policy_other = lax.ppermute(policy_send, DP_MP, pairs)
    reference_other = lax.ppermute(reference_send, DP_MP, pairs)

    weights = mixture_weight.reshape(shards, 2, part)
    tokens = sampled_tokens.reshape(shards, 2, part)
    weight = lax.dynamic_index_in_dim(weights, half, 1, False).reshape(1, shards * part)
    token = lax.dynamic_index_in_dim(tokens, half, 1, False).reshape(1, shards * part)
    token = jnp.concatenate([token - first_own, token - first_other])
    diff_own, diff_send, sums = mixture(
        hidden, policy_embedding, policy_other, reference_embedding, reference_other, weight, token
    )
    diff_other = lax.ppermute(diff_send, DP_MP, pairs)

    seqs = shards * part
    sums = jnp.sum(everywhere(sums.reshape(1, 5 * seqs), DP), axis=0).reshape(5, shards, part)
    mine = lax.dynamic_index_in_dim(sums[2:], shard, 1, False)
    block = jnp.concatenate(
        [sums[:2].reshape(1, 2 * seqs), mine.reshape(1, 3 * part), jnp.zeros((1, part), jnp.float32)],
        axis=1,
    )
    blocks = everywhere(block, MP)
    index = jnp.arange(copies, dtype=jnp.int32)
    parity = (index // lax.axis_size("mp_1") + index % lax.axis_size("mp_1")) % 2
    by_half = [
        jnp.sum(jnp.where((parity == k)[:, None, None], blocks, 0.0), axis=0)[0] for k in range(2)
    ]
    totals = jnp.stack([b[: 2 * seqs] for b in by_half]).reshape(2, 2, shards, part)
    side = jnp.stack([b[2 * seqs : 2 * seqs + 3 * part] for b in by_half]).reshape(2, 3, part)
    logs = jnp.log(totals)
    delta = (logs[:, 0] - logs[:, 1]).reshape(2, seqs)
    delta = jnp.where(half == 0, delta, delta[::-1])
    mixture_shift = shift(half_arg, diff_own, diff_other, delta, shards)

    log_mine = lax.dynamic_index_in_dim(logs, shard, 2, False)
    weight_mine = lax.dynamic_index_in_dim(weights, shard, 0, False)
    policy_pick = side[:, 1]
    reference_pick = side[:, 2]
    mixed_pick = (1.0 - weight_mine) * policy_pick + weight_mine * reference_pick
    sampled_logprobs = jnp.stack(
        [
            (policy_pick - log_mine[:, 0]).reshape(seq_local),
            (reference_pick - jnp.log(side[:, 0])).reshape(seq_local),
            (mixed_pick - log_mine[:, 1]).reshape(seq_local),
        ]
    )
    return (mixture_shift.reshape(shards * seq_local, vocab), sampled_logprobs)


def solution(mesh):
    split = Mesh(mesh.devices.reshape(8, 2, 8, 4), ("dp_0", "dp_1", "mp_0", "mp_1"))
    in_specs = (P(DP, None), P(DP, None), P(), P(), P(DP_MP, None), P(DP_MP, None), P(), P())
    out_specs = (P(None, DP_MP), P(None, DP))
    return jax.shard_map(local, mesh=split, in_specs=in_specs, out_specs=out_specs, check_vma=False)
```

```python
import functools

import jax
import jax.numpy as jnp
from jax import lax
from jax.experimental import pallas as pl
from jax.experimental.pallas import tpu as pltpu
from jax.sharding import Mesh
from jax.sharding import PartitionSpec as P

DP = ("dp_0", "dp_1")
MP = ("mp_0", "mp_1")
DP_MP = ("dp_0", "dp_1", "mp_0", "mp_1")

softcap = 30.0
epsilon = 1e-06

MIB = 1024 * 1024
HBM = pl.BlockSpec(memory_space=pltpu.HBM)
VMEM = pl.BlockSpec(memory_space=pltpu.VMEM)


def in_hbm(x):
    return pltpu.with_memory_space_constraint(x, pltpu.HBM)


def normalize_kernel(half_ref, policy_ref, reference_ref, policy_gain_ref, reference_gain_ref, out_ref, rows, in_sem):
    part = out_ref.shape[1]
    first = pl.multiple_of(half_ref[0] * part, part)
    models = ((policy_ref, policy_gain_ref), (reference_ref, reference_gain_ref))
    loads = [
        pltpu.make_async_copy(hidden_ref.at[pl.ds(first, part), :], rows.at[model], in_sem.at[model])
        for model, (hidden_ref, _) in enumerate(models)
    ]
    for load in loads:
        load.start()
    for model, (_, gain_ref) in enumerate(models):
        loads[model].wait()
        values = rows[model].astype(jnp.float32)
        meansq = jnp.mean(values * values, axis=-1, keepdims=True)
        gain = gain_ref[...].reshape(1, values.shape[1])
        normed = values * lax.rsqrt(meansq + epsilon) * gain
        out_ref[model] = normed.astype(jnp.bfloat16)


def normalize(half, policy_hidden, reference_hidden, policy_gain, reference_gain):
    rows, width = policy_hidden.shape
    part = rows // 2
    return pl.pallas_call(
        normalize_kernel,
        in_specs=[pl.BlockSpec(memory_space=pltpu.SMEM)] + [HBM] * 2 + [VMEM] * 2,
        out_specs=VMEM,
        out_shape=jax.ShapeDtypeStruct((2, part, width), jnp.bfloat16),
        scratch_shapes=[pltpu.VMEM((2, part, width), jnp.bfloat16), pltpu.SemaphoreType.DMA((2,))],
        compiler_params=pltpu.CompilerParams(vmem_limit_bytes=16 * MIB),
        name="normalize",
    )(half, in_hbm(policy_hidden), in_hbm(reference_hidden), in_hbm(policy_gain), in_hbm(reference_gain))


def stage_kernel(policy_own, policy_other, reference_own, reference_other, out_ref, sem):
    copies = [
        pltpu.make_async_copy(rows_ref, out_ref.at[place], sem.at[place])
        for place, rows_ref in enumerate((policy_own, policy_other, reference_own, reference_other))
    ]
    for copy in copies:
        copy.start()
    for copy in copies:
        copy.wait()


def stage(*embeddings):
    return pl.pallas_call(
        stage_kernel,
        in_specs=[HBM] * 4,
        out_specs=VMEM,
        out_shape=pltpu.VMEM((4,) + embeddings[0].shape, jnp.bfloat16),
        scratch_shapes=[pltpu.SemaphoreType.DMA((4,))],
        compiler_params=pltpu.CompilerParams(vmem_limit_bytes=16 * MIB),
        name="stage",
    )(*map(in_hbm, embeddings))


def mixture_kernel(
    hidden_ref,
    rows_ref,
    weight_ref,
    token_ref,
    diff_own_ref,
    diff_other_ref,
    block_ref,
    hidden,
    policy_acc,
    reference_acc,
    partial,
    sem,
):
    chunks = sem.shape[0]
    shards, _, part, width = hidden_ref.shape
    depth = width // chunks
    vocab = rows_ref.shape[1]
    seqs = shards * part

    def load(k):
        columns = pl.ds(k * depth, depth)
        return pltpu.make_async_copy(
            hidden_ref.at[:, :, :, columns], hidden.at[:, :, :, columns], sem.at[k]
        )

    for k in range(chunks):
        load(k).start()
    for k in range(chunks):
        load(k).wait()
        columns = pl.ds(k * depth, depth)
        for model, acc in enumerate((policy_acc, reference_acc)):
            left = hidden[:, model, :, columns].reshape(seqs, depth)
            for place in range(2):
                product = lax.dot_general(
                    left,
                    rows_ref[2 * model + place, :, columns],
                    (((1,), (1,)), ((), ())),
                    preferred_element_type=jnp.float32,
                )
                target = pl.ds(place * vocab, vocab)
                acc[:, target] = product if k == 0 else acc[:, target] + product

    def body(i, carry):
        rows = pl.ds(pl.multiple_of(i * 8, 8), 8)
        weight = weight_ref[rows, :]
        keep = 1.0 - weight
        sums = [jnp.zeros((8, 128), jnp.float32) for _ in range(5)]
        for place, diff_ref in enumerate((diff_own_ref, diff_other_ref)):
            token = token_ref[place, rows, :]
            for group in range(vocab // 128):
                lanes = pl.ds(place * vocab + group * 128, 128)
                policy = softcap * jnp.tanh(policy_acc[rows, lanes] * (1.0 / softcap))
                reference = softcap * jnp.tanh(reference_acc[rows, lanes] * (1.0 / softcap))
                mixed = keep * policy + weight * reference
                diff_ref[rows, pl.ds(group * 128, 128)] = mixed - policy
                hit = lax.broadcasted_iota(jnp.int32, (8, 128), 1) + group * 128 == token
                terms = (
                    jnp.exp(policy),
                    jnp.exp(mixed),
                    jnp.exp(reference),
                    jnp.where(hit, policy, 0.0),
                    jnp.where(hit, reference, 0.0),
                )
                sums = [total + term for total, term in zip(sums, terms)]
        for k in range(5):
            partial[k, rows, :] = sums[k]
        return carry

    lax.fori_loop(0, seqs // 8, body, 0, unroll=2)
    sums = [jnp.sum(partial[k].T, axis=0, keepdims=True) for k in range(5)]
    whole = jnp.concatenate(sums[:2], axis=1)
    for shard in range(shards):
        start = shard * part // 128 * 128
        block_ref[shard] = jnp.concatenate(
            [whole] + [total[:, start : start + 128] for total in sums[2:]], axis=1
        )


def mixture(hidden, rows, weight, token):
    shards, _, part, width = hidden.shape
    vocab = rows.shape[1]
    seqs = shards * part
    chunks = 7
    return pl.pallas_call(
        mixture_kernel,
        in_specs=[HBM] + [VMEM] * 3,
        out_specs=[VMEM] * 3,
        out_shape=[
            jax.ShapeDtypeStruct((seqs, vocab), jnp.float32),
            jax.ShapeDtypeStruct((seqs, vocab), jnp.float32),
            jax.ShapeDtypeStruct((shards, 1, 2 * seqs + 3 * 128), jnp.float32),
        ],
        scratch_shapes=[
            pltpu.VMEM((shards, 2, part, width), jnp.bfloat16),
            pltpu.VMEM((seqs, 2 * vocab), jnp.float32),
            pltpu.VMEM((seqs, 2 * vocab), jnp.float32),
            pltpu.VMEM((5, seqs, 128), jnp.float32),
            pltpu.SemaphoreType.DMA((chunks,)),
        ],
        compiler_params=pltpu.CompilerParams(vmem_limit_bytes=32 * MIB),
        name="mixture",
    )(in_hbm(hidden), pltpu.with_memory_space_constraint(rows, pltpu.VMEM), weight, token)


def finish_kernel(columns, place_ref, own_ref, other_ref, blocks_ref, weight_ref, shift_ref, sampled_ref, staged, sem):
    shards, _, part, vocab = shift_ref.shape
    seqs = shards * part
    half = place_ref[0]
    shard = place_ref[1]

    totals = [None, None]
    for j in range(blocks_ref.shape[0]):
        k = (j // columns + j % columns) % 2
        totals[k] = blocks_ref[j] if totals[k] is None else totals[k] + blocks_ref[j]
    logs = [jnp.log(total[:, : 2 * seqs + 128]) for total in totals]
    deltas = [log[:, :seqs] - log[:, seqs : 2 * seqs] for log in logs]
    own_first = half == 0
    turns = (
        jnp.where(own_first, deltas[0], deltas[1]),
        jnp.where(own_first, deltas[1], deltas[0]),
    )

    chunk = 128
    per = chunk // part
    stores = []
    for turn, diff_ref in enumerate((own_ref, other_ref)):
        target = half if turn == 0 else 1 - half
        for j in range(seqs // chunk):
            delta = jnp.broadcast_to(turns[turn][:, j * chunk : (j + 1) * chunk], (chunk, chunk)).T
            shards_here = pl.ds(j * per, per)
            for group in range(vocab // 128):
                lanes = pl.ds(group * 128, 128)
                shifted = diff_ref[pl.ds(j * chunk, chunk), lanes] + delta
                staged[turn, shards_here, :, lanes] = shifted.reshape(per, part, 128)
            store = pltpu.make_async_copy(
                staged.at[turn, shards_here],
                shift_ref.at[shards_here, target],
                sem.at[turn, j],
            )
            store.start()
            stores.append(store)

    mine = shard * part // 128
    picked = []
    for total, log in zip(totals, logs):
        policy = jnp.zeros((1, 128), jnp.float32)
        mixed = jnp.zeros((1, 128), jnp.float32)
        for j in range(seqs // 128):
            policy = jnp.where(mine == j, log[:, j * 128 : (j + 1) * 128], policy)
            mixed = jnp.where(mine == j, log[:, seqs + j * 128 : seqs + (j + 1) * 128], mixed)
        policy_pick = total[:, 2 * seqs + 128 : 2 * seqs + 256]
        reference_pick = total[:, 2 * seqs + 256 : 2 * seqs + 384]
        picked.append((policy_pick, reference_pick, policy, log[:, 2 * seqs :], mixed))
    lane = lax.broadcasted_iota(jnp.int32, (8, 128), 1)
    start = shard * part % 128
    values = []
    for low, high in zip(*picked):
        low = pltpu.roll(jnp.broadcast_to(low, (8, 128)), lax.rem(128 - start, 128), 1)
        high = pltpu.roll(jnp.broadcast_to(high, (8, 128)), lax.rem(128 + part - start, 128), 1)
        values.append(jnp.where(lane < part, low, high)[:1, : 2 * part])
    policy_pick, reference_pick, policy_log, reference_log, mixed_log = values
    weight = weight_ref[...]
    sampled_ref[0:1, :] = policy_pick - policy_log
    sampled_ref[1:2, :] = reference_pick - reference_log
    sampled_ref[2:3, :] = (1.0 - weight) * policy_pick + weight * reference_pick - mixed_log

    for store in stores:
        store.wait()


def finish(place, columns, diff_own, diff_other, blocks, weight, shards):
    seqs, vocab = diff_own.shape
    part = seqs // shards
    return pl.pallas_call(
        functools.partial(finish_kernel, columns),
        in_specs=[pl.BlockSpec(memory_space=pltpu.SMEM)] + [VMEM] * 4,
        out_specs=[HBM, VMEM],
        out_shape=[
            jax.ShapeDtypeStruct((shards, 2, part, vocab), jnp.float32),
            jax.ShapeDtypeStruct((3, 2 * part), jnp.float32),
        ],
        scratch_shapes=[
            pltpu.VMEM((2, shards, part, vocab), jnp.float32),
            pltpu.SemaphoreType.DMA((2, seqs // 128)),
        ],
        compiler_params=pltpu.CompilerParams(vmem_limit_bytes=16 * MIB),
        name="finish",
    )(place, diff_own, diff_other, blocks, weight)


def partners(z, y, x):
    pairs = []
    for source in range(z * 2 * y * x):
        i, rest = divmod(source, 2 * y * x)
        c, rest = divmod(rest, y * x)
        j, k = divmod(rest, x)
        j, k = (j, k ^ 1) if c == 0 else (j ^ 1, k)
        pairs.append((source, ((i * 2 + c) * y + j) * x + k))
    return pairs


def local(
    policy_hidden,
    reference_hidden,
    policy_gain,
    reference_gain,
    policy_embedding,
    reference_embedding,
    mixture_weight,
    sampled_tokens,
):
    seq_local = policy_hidden.shape[0]
    part = seq_local // 2
    vocab = policy_embedding.shape[0]
    shards = lax.axis_size(DP)
    copies = lax.axis_size(MP)
    shard = lax.axis_index(DP)
    copy = lax.axis_index(MP)
    core = lax.axis_index("dp_1")
    row = lax.axis_index("mp_0")
    column = lax.axis_index("mp_1")
    half = (row + column) % 2
    other_copy = jnp.where(
        core == 0,
        row * lax.axis_size("mp_1") + (column ^ 1),
        (row ^ 1) * lax.axis_size("mp_1") + column,
    )
    first_own = (shard * copies + copy) * vocab
    first_other = (shard * copies + other_copy) * vocab
    place = jnp.stack([half, shard]).astype(jnp.int32)
    pairs = partners(lax.axis_size("dp_0"), lax.axis_size("mp_0"), lax.axis_size("mp_1"))

    normed = normalize(place, policy_hidden, reference_hidden, policy_gain, reference_gain)
    normed, policy_send, reference_send = lax.optimization_barrier(
        (normed, policy_embedding, reference_embedding)
    )
    hidden = lax.all_gather(normed, DP, axis=0)
    policy_other = lax.ppermute(policy_send, DP_MP, pairs)
    reference_other = lax.ppermute(reference_send, DP_MP, pairs)

    seqs = shards * part
    weights = mixture_weight.reshape(shards, 2, part)
    tokens = sampled_tokens.reshape(shards, 2, part)
    weight = lax.dynamic_index_in_dim(weights, half, 1, False).reshape(seqs, 1)
    token = lax.dynamic_index_in_dim(tokens, half, 1, False).reshape(seqs, 1)
    token = jnp.stack([token - first_own, token - first_other])
    weight = jnp.broadcast_to(weight, (seqs, 128))
    token = jnp.broadcast_to(token, (2, seqs, 128))
    weight_mine = lax.dynamic_slice_in_dim(mixture_weight, shard * seq_local, seq_local)[None]
    policy_other, reference_other, weight, token = lax.optimization_barrier(
        (policy_other, reference_other, weight, token)
    )
    rows = stage(policy_embedding, policy_other, reference_embedding, reference_other)
    diff_own, diff_send, block = mixture(hidden, rows, weight, token)
    diff_other = lax.ppermute(diff_send, DP_MP, pairs)

    block = jnp.sum(lax.all_to_all(block, DP, 0, 0, tiled=True), axis=0, keepdims=True)
    block = jnp.broadcast_to(block, (copies,) + block.shape[1:])
    blocks = lax.all_to_all(block, MP, 0, 0, tiled=True)
    mixture_shift, sampled_logprobs = finish(
        place, lax.axis_size("mp_1"), diff_own, diff_other, blocks, weight_mine, shards
    )
    return (mixture_shift.reshape(shards * seq_local, vocab), sampled_logprobs)


def solution(mesh):
    split = Mesh(mesh.devices.reshape(8, 2, 8, 4), ("dp_0", "dp_1", "mp_0", "mp_1"))
    in_specs = (P(DP, None), P(DP, None), P(), P(), P(DP_MP, None), P(DP_MP, None), P(), P())
    out_specs = (P(None, DP_MP), P(None, DP))
    return jax.shard_map(local, mesh=split, in_specs=in_specs, out_specs=out_specs, check_vma=False)
```

```python
import functools

import jax
import jax.numpy as jnp
from jax import lax
from jax.experimental import pallas as pl
from jax.experimental.pallas import tpu as pltpu
from jax.sharding import Mesh
from jax.sharding import PartitionSpec as P

DP = ("dp_0", "dp_1")
MP = ("mp_0", "mp_1")
DP_MP = ("dp_0", "dp_1", "mp_0", "mp_1")

softcap = 30.0
epsilon = 1e-06

MIB = 1024 * 1024
HBM = pl.BlockSpec(memory_space=pltpu.HBM)
VMEM = pl.BlockSpec(memory_space=pltpu.VMEM)


def in_hbm(x):
    return pltpu.with_memory_space_constraint(x, pltpu.HBM)


def normalize_kernel(half_ref, policy_ref, reference_ref, policy_gain_ref, reference_gain_ref, out_ref, rows, in_sem):
    part = out_ref.shape[1]
    first = pl.multiple_of(half_ref[0] * part, part)
    models = ((policy_ref, policy_gain_ref), (reference_ref, reference_gain_ref))
    loads = [
        pltpu.make_async_copy(hidden_ref.at[pl.ds(first, part), :], rows.at[model], in_sem.at[model])
        for model, (hidden_ref, _) in enumerate(models)
    ]
    for load in loads:
        load.start()
    for model, (_, gain_ref) in enumerate(models):
        loads[model].wait()
        values = rows[model].astype(jnp.float32)
        meansq = jnp.mean(values * values, axis=-1, keepdims=True)
        gain = gain_ref[...].reshape(1, values.shape[1])
        normed = values * lax.rsqrt(meansq + epsilon) * gain
        out_ref[model] = normed.astype(jnp.bfloat16)


def normalize(half, policy_hidden, reference_hidden, policy_gain, reference_gain):
    rows, width = policy_hidden.shape
    part = rows // 2
    return pl.pallas_call(
        normalize_kernel,
        in_specs=[pl.BlockSpec(memory_space=pltpu.SMEM)] + [HBM] * 2 + [VMEM] * 2,
        out_specs=VMEM,
        out_shape=jax.ShapeDtypeStruct((2, part, width), jnp.bfloat16),
        scratch_shapes=[pltpu.VMEM((2, part, width), jnp.bfloat16), pltpu.SemaphoreType.DMA((2,))],
        compiler_params=pltpu.CompilerParams(vmem_limit_bytes=16 * MIB),
        name="normalize",
    )(half, in_hbm(policy_hidden), in_hbm(reference_hidden), in_hbm(policy_gain), in_hbm(reference_gain))


def mixture_kernel(
    hidden_ref,
    policy_own_ref,
    policy_other_ref,
    reference_own_ref,
    reference_other_ref,
    weight_ref,
    token_ref,
    diff_own_ref,
    diff_other_ref,
    block_ref,
    hidden,
    loaded,
    policy_acc,
    reference_acc,
    partial,
    sem,
):
    chunks = sem.shape[0]
    shards, _, part, width = hidden_ref.shape
    depth = width // chunks
    vocab = policy_own_ref.shape[0]
    seqs = shards * part

    def loads(k):
        columns = pl.ds(k * depth, depth)
        rest = (policy_other_ref, reference_own_ref, reference_other_ref)
        pairs = [(hidden_ref.at[:, :, :, columns], hidden.at[:, :, :, columns])]
        pairs += [(ref.at[:, columns], loaded.at[i, :, columns]) for i, ref in enumerate(rest)]
        return [pltpu.make_async_copy(*pair, sem.at[k, i]) for i, pair in enumerate(pairs)]

    for k in range(chunks):
        for load in loads(k):
            load.start()
    for k in range(chunks):
        for load in loads(k):
            load.wait()
        columns = pl.ds(k * depth, depth)
        for model, acc in enumerate((policy_acc, reference_acc)):
            left = hidden[:, model, :, columns].reshape(seqs, depth)
            for place in range(2):
                index = 2 * model + place
                rows = policy_own_ref[:, columns] if index == 0 else loaded[index - 1, :, columns]
                product = lax.dot_general(
                    left, rows, (((1,), (1,)), ((), ())), preferred_element_type=jnp.float32
                )
                target = pl.ds(place * vocab, vocab)
                acc[:, target] = product if k == 0 else acc[:, target] + product

    def body(i, carry):
        rows = pl.ds(pl.multiple_of(i * 8, 8), 8)
        weight = weight_ref[rows, :]
        keep = 1.0 - weight
        sums = [jnp.zeros((8, 128), jnp.float32) for _ in range(5)]
        for place, diff_ref in enumerate((diff_own_ref, diff_other_ref)):
            token = token_ref[place, rows, :]
            for group in range(vocab // 128):
                lanes = pl.ds(place * vocab + group * 128, 128)
                policy = softcap * jnp.tanh(policy_acc[rows, lanes] * (1.0 / softcap))
                reference = softcap * jnp.tanh(reference_acc[rows, lanes] * (1.0 / softcap))
                mixed = keep * policy + weight * reference
                diff_ref[rows, pl.ds(group * 128, 128)] = mixed - policy
                hit = lax.broadcasted_iota(jnp.int32, (8, 128), 1) + group * 128 == token
                terms = (
                    jnp.exp(policy),
                    jnp.exp(mixed),
                    jnp.exp(reference),
                    jnp.where(hit, policy, 0.0),
                    jnp.where(hit, reference, 0.0),
                )
                sums = [total + term for total, term in zip(sums, terms)]
        for k in range(5):
            partial[k, rows, :] = sums[k]
        return carry

    lax.fori_loop(0, seqs // 8, body, 0, unroll=2)
    sums = [jnp.sum(partial[k].T, axis=0, keepdims=True) for k in range(5)]
    whole = jnp.concatenate(sums[:2], axis=1)
    for shard in range(shards):
        start = shard * part // 128 * 128
        block_ref[shard] = jnp.concatenate(
            [whole] + [total[:, start : start + 128] for total in sums[2:]], axis=1
        )


def mixture(hidden, policy_own, policy_other, reference_own, reference_other, weight, token):
    shards, _, part, width = hidden.shape
    vocab = policy_own.shape[0]
    seqs = shards * part
    chunks = 7
    return pl.pallas_call(
        mixture_kernel,
        in_specs=[HBM, VMEM] + [HBM] * 3 + [VMEM] * 2,
        out_specs=[VMEM] * 3,
        out_shape=[
            jax.ShapeDtypeStruct((seqs, vocab), jnp.float32),
            jax.ShapeDtypeStruct((seqs, vocab), jnp.float32),
            jax.ShapeDtypeStruct((shards, 1, 2 * seqs + 3 * 128), jnp.float32),
        ],
        scratch_shapes=[
            pltpu.VMEM((shards, 2, part, width), jnp.bfloat16),
            pltpu.VMEM((3, vocab, width), jnp.bfloat16),
            pltpu.VMEM((seqs, 2 * vocab), jnp.float32),
            pltpu.VMEM((seqs, 2 * vocab), jnp.float32),
            pltpu.VMEM((5, seqs, 128), jnp.float32),
            pltpu.SemaphoreType.DMA((chunks, 4)),
        ],
        compiler_params=pltpu.CompilerParams(vmem_limit_bytes=32 * MIB),
        name="mixture",
    )(
        in_hbm(hidden),
        pltpu.with_memory_space_constraint(policy_own, pltpu.VMEM),
        in_hbm(policy_other),
        in_hbm(reference_own),
        in_hbm(reference_other),
        weight,
        token,
    )


def finish_kernel(columns, place_ref, own_ref, other_ref, blocks_ref, weight_ref, shift_ref, sampled_ref, staged, sem):
    shards, _, part, vocab = shift_ref.shape
    seqs = shards * part
    half = place_ref[0]
    shard = place_ref[1]

    totals = [None, None]
    for j in range(blocks_ref.shape[0]):
        k = (j // columns + j % columns) % 2
        totals[k] = blocks_ref[j] if totals[k] is None else totals[k] + blocks_ref[j]
    logs = [jnp.log(total[:, : 2 * seqs + 128]) for total in totals]
    deltas = [log[:, :seqs] - log[:, seqs : 2 * seqs] for log in logs]
    own_first = half == 0
    turns = (
        jnp.where(own_first, deltas[0], deltas[1]),
        jnp.where(own_first, deltas[1], deltas[0]),
    )

    chunk = 128
    per = chunk // part
    stores = []
    for turn, diff_ref in enumerate((own_ref, other_ref)):
        target = half if turn == 0 else 1 - half
        for j in range(seqs // chunk):
            delta = jnp.broadcast_to(turns[turn][:, j * chunk : (j + 1) * chunk], (chunk, chunk)).T
            shards_here = pl.ds(j * per, per)
            for group in range(vocab // 128):
                lanes = pl.ds(group * 128, 128)
                shifted = diff_ref[pl.ds(j * chunk, chunk), lanes] + delta
                staged[turn, shards_here, :, lanes] = shifted.reshape(per, part, 128)
            store = pltpu.make_async_copy(
                staged.at[turn, shards_here],
                shift_ref.at[shards_here, target],
                sem.at[turn, j],
            )
            store.start()
            stores.append(store)

    mine = shard * part // 128
    picked = []
    for total, log in zip(totals, logs):
        policy = jnp.zeros((1, 128), jnp.float32)
        mixed = jnp.zeros((1, 128), jnp.float32)
        for j in range(seqs // 128):
            policy = jnp.where(mine == j, log[:, j * 128 : (j + 1) * 128], policy)
            mixed = jnp.where(mine == j, log[:, seqs + j * 128 : seqs + (j + 1) * 128], mixed)
        policy_pick = total[:, 2 * seqs + 128 : 2 * seqs + 256]
        reference_pick = total[:, 2 * seqs + 256 : 2 * seqs + 384]
        picked.append((policy_pick, reference_pick, policy, log[:, 2 * seqs :], mixed))
    lane = lax.broadcasted_iota(jnp.int32, (8, 128), 1)
    start = shard * part % 128
    values = []
    for low, high in zip(*picked):
        low = pltpu.roll(jnp.broadcast_to(low, (8, 128)), lax.rem(128 - start, 128), 1)
        high = pltpu.roll(jnp.broadcast_to(high, (8, 128)), lax.rem(128 + part - start, 128), 1)
        values.append(jnp.where(lane < part, low, high)[:1, : 2 * part])
    policy_pick, reference_pick, policy_log, reference_log, mixed_log = values
    weight = weight_ref[...]
    sampled_ref[0:1, :] = policy_pick - policy_log
    sampled_ref[1:2, :] = reference_pick - reference_log
    sampled_ref[2:3, :] = (1.0 - weight) * policy_pick + weight * reference_pick - mixed_log

    for store in stores:
        store.wait()


def finish(place, columns, diff_own, diff_other, blocks, weight, shards):
    seqs, vocab = diff_own.shape
    part = seqs // shards
    return pl.pallas_call(
        functools.partial(finish_kernel, columns),
        in_specs=[pl.BlockSpec(memory_space=pltpu.SMEM)] + [VMEM] * 4,
        out_specs=[HBM, VMEM],
        out_shape=[
            jax.ShapeDtypeStruct((shards, 2, part, vocab), jnp.float32),
            jax.ShapeDtypeStruct((3, 2 * part), jnp.float32),
        ],
        scratch_shapes=[
            pltpu.VMEM((2, shards, part, vocab), jnp.float32),
            pltpu.SemaphoreType.DMA((2, seqs // 128)),
        ],
        compiler_params=pltpu.CompilerParams(vmem_limit_bytes=16 * MIB),
        name="finish",
    )(place, diff_own, diff_other, blocks, weight)


def partners(z, y, x):
    pairs = []
    for source in range(z * 2 * y * x):
        i, rest = divmod(source, 2 * y * x)
        c, rest = divmod(rest, y * x)
        j, k = divmod(rest, x)
        j, k = (j, k ^ 1) if c == 0 else (j ^ 1, k)
        pairs.append((source, ((i * 2 + c) * y + j) * x + k))
    return pairs


def local(
    policy_hidden,
    reference_hidden,
    policy_gain,
    reference_gain,
    policy_embedding,
    reference_embedding,
    mixture_weight,
    sampled_tokens,
):
    seq_local = policy_hidden.shape[0]
    part = seq_local // 2
    vocab = policy_embedding.shape[0]
    shards = lax.axis_size(DP)
    copies = lax.axis_size(MP)
    shard = lax.axis_index(DP)
    copy = lax.axis_index(MP)
    core = lax.axis_index("dp_1")
    row = lax.axis_index("mp_0")
    column = lax.axis_index("mp_1")
    half = (row + column) % 2
    other_copy = jnp.where(
        core == 0,
        row * lax.axis_size("mp_1") + (column ^ 1),
        (row ^ 1) * lax.axis_size("mp_1") + column,
    )
    first_own = (shard * copies + copy) * vocab
    first_other = (shard * copies + other_copy) * vocab
    place = jnp.stack([half, shard]).astype(jnp.int32)
    pairs = partners(lax.axis_size("dp_0"), lax.axis_size("mp_0"), lax.axis_size("mp_1"))

    normed = normalize(place, policy_hidden, reference_hidden, policy_gain, reference_gain)
    normed, policy_send, reference_send = lax.optimization_barrier(
        (normed, policy_embedding, reference_embedding)
    )
    hidden = lax.all_gather(normed, DP, axis=0)
    policy_other = lax.ppermute(policy_send, DP_MP, pairs)
    reference_other = lax.ppermute(reference_send, DP_MP, pairs)

    seqs = shards * part
    weights = mixture_weight.reshape(shards, 2, part)
    tokens = sampled_tokens.reshape(shards, 2, part)
    weight = lax.dynamic_index_in_dim(weights, half, 1, False).reshape(seqs, 1)
    token = lax.dynamic_index_in_dim(tokens, half, 1, False).reshape(seqs, 1)
    token = jnp.stack([token - first_own, token - first_other])
    weight = jnp.broadcast_to(weight, (seqs, 128))
    token = jnp.broadcast_to(token, (2, seqs, 128))
    weight_mine = lax.dynamic_slice_in_dim(mixture_weight, shard * seq_local, seq_local)[None]
    policy_other, reference_other, weight, token = lax.optimization_barrier(
        (policy_other, reference_other, weight, token)
    )
    diff_own, diff_send, block = mixture(
        hidden, policy_embedding, policy_other, reference_embedding, reference_other, weight, token
    )

    block = lax.all_to_all(block, DP, 0, 0, tiled=True)
    block, diff_send = lax.optimization_barrier((block, diff_send))
    diff_other = lax.ppermute(diff_send, DP_MP, pairs)
    block = jnp.sum(block, axis=0, keepdims=True)
    block = jnp.broadcast_to(block, (copies,) + block.shape[1:])
    blocks = lax.all_to_all(block, MP, 0, 0, tiled=True)
    mixture_shift, sampled_logprobs = finish(
        place, lax.axis_size("mp_1"), diff_own, diff_other, blocks, weight_mine, shards
    )
    return (mixture_shift.reshape(shards * seq_local, vocab), sampled_logprobs)


def solution(mesh):
    split = Mesh(mesh.devices.reshape(8, 2, 8, 4), ("dp_0", "dp_1", "mp_0", "mp_1"))
    in_specs = (P(DP, None), P(DP, None), P(), P(), P(DP_MP, None), P(DP_MP, None), P(), P())
    out_specs = (P(None, DP_MP), P(None, DP))
    return jax.shard_map(local, mesh=split, in_specs=in_specs, out_specs=out_specs, check_vma=False)
```

```python
import functools

import jax
import jax.numpy as jnp
from jax import lax
from jax.experimental import pallas as pl
from jax.experimental.pallas import tpu as pltpu
from jax.sharding import Mesh
from jax.sharding import PartitionSpec as P

DP = ("dp_0", "dp_1")
MP = ("mp_0", "mp_1")
DP_MP = ("dp_0", "dp_1", "mp_0", "mp_1")

softcap = 30.0
epsilon = 1e-06

MIB = 1024 * 1024
HBM = pl.BlockSpec(memory_space=pltpu.HBM)
VMEM = pl.BlockSpec(memory_space=pltpu.VMEM)


def in_hbm(x):
    return pltpu.with_memory_space_constraint(x, pltpu.HBM)


def normalize_kernel(half_ref, policy_ref, reference_ref, policy_gain_ref, reference_gain_ref, out_ref, rows, in_sem):
    part = out_ref.shape[1]
    first = pl.multiple_of(half_ref[0] * part, part)
    models = ((policy_ref, policy_gain_ref), (reference_ref, reference_gain_ref))
    loads = [
        pltpu.make_async_copy(hidden_ref.at[pl.ds(first, part), :], rows.at[model], in_sem.at[model])
        for model, (hidden_ref, _) in enumerate(models)
    ]
    for load in loads:
        load.start()
    for model, (_, gain_ref) in enumerate(models):
        loads[model].wait()
        values = rows[model].astype(jnp.float32)
        meansq = jnp.mean(values * values, axis=-1, keepdims=True)
        gain = gain_ref[...].reshape(1, values.shape[1])
        normed = values * lax.rsqrt(meansq + epsilon) * gain
        out_ref[model] = normed.astype(jnp.bfloat16)


def normalize(half, policy_hidden, reference_hidden, policy_gain, reference_gain):
    rows, width = policy_hidden.shape
    part = rows // 2
    return pl.pallas_call(
        normalize_kernel,
        in_specs=[pl.BlockSpec(memory_space=pltpu.SMEM)] + [HBM] * 2 + [VMEM] * 2,
        out_specs=VMEM,
        out_shape=jax.ShapeDtypeStruct((2, part, width), jnp.bfloat16),
        scratch_shapes=[pltpu.VMEM((2, part, width), jnp.bfloat16), pltpu.SemaphoreType.DMA((2,))],
        compiler_params=pltpu.CompilerParams(vmem_limit_bytes=16 * MIB),
        name="normalize",
    )(half, in_hbm(policy_hidden), in_hbm(reference_hidden), in_hbm(policy_gain), in_hbm(reference_gain))


def mixture_kernel(
    hidden_ref,
    policy_own_ref,
    policy_other_ref,
    reference_own_ref,
    reference_other_ref,
    weight_ref,
    token_ref,
    diff_own_ref,
    diff_other_ref,
    block_ref,
    hidden,
    loaded,
    policy_acc,
    reference_acc,
    partial,
    sem,
):
    chunks = sem.shape[0]
    shards, _, part, width = hidden_ref.shape
    depth = width // chunks
    vocab = policy_own_ref.shape[0]
    seqs = shards * part

    def loads(k):
        columns = pl.ds(k * depth, depth)
        rest = (policy_other_ref, reference_own_ref, reference_other_ref)
        pairs = [(hidden_ref.at[:, :, :, columns], hidden.at[:, :, :, columns])]
        pairs += [(ref.at[:, columns], loaded.at[i, :, columns]) for i, ref in enumerate(rest)]
        return [pltpu.make_async_copy(*pair, sem.at[k, i]) for i, pair in enumerate(pairs)]

    for k in range(chunks):
        for load in loads(k):
            load.start()
    for k in range(chunks):
        for load in loads(k):
            load.wait()
        columns = pl.ds(k * depth, depth)
        for model, acc in enumerate((policy_acc, reference_acc)):
            left = hidden[:, model, :, columns].reshape(seqs, depth)
            for place in range(2):
                index = 2 * model + place
                rows = policy_own_ref[:, columns] if index == 0 else loaded[index - 1, :, columns]
                product = lax.dot_general(
                    left, rows, (((1,), (1,)), ((), ())), preferred_element_type=jnp.float32
                )
                target = pl.ds(place * vocab, vocab)
                acc[:, target] = product if k == 0 else acc[:, target] + product

    def body(i, carry):
        rows = pl.ds(pl.multiple_of(i * 8, 8), 8)
        weight = weight_ref[rows, :]
        keep = 1.0 - weight
        sums = [jnp.zeros((8, 128), jnp.float32) for _ in range(5)]
        for place, diff_ref in enumerate((diff_own_ref, diff_other_ref)):
            token = token_ref[place, rows, :]
            for group in range(vocab // 128):
                lanes = pl.ds(place * vocab + group * 128, 128)
                policy = softcap * jnp.tanh(policy_acc[rows, lanes] * (1.0 / softcap))
                reference = softcap * jnp.tanh(reference_acc[rows, lanes] * (1.0 / softcap))
                mixed = keep * policy + weight * reference
                diff_ref[rows, pl.ds(group * 128, 128)] = mixed - policy
                hit = lax.broadcasted_iota(jnp.int32, (8, 128), 1) + group * 128 == token
                terms = (
                    jnp.exp(policy),
                    jnp.exp(mixed),
                    jnp.exp(reference),
                    jnp.where(hit, policy, 0.0),
                    jnp.where(hit, reference, 0.0),
                )
                sums = [total + term for total, term in zip(sums, terms)]
        for k in range(5):
            partial[k, rows, :] = sums[k]
        return carry

    lax.fori_loop(0, seqs // 8, body, 0, unroll=8)
    sums = [jnp.sum(partial[k].T, axis=0, keepdims=True) for k in range(5)]
    whole = jnp.concatenate(sums[:2], axis=1)
    for shard in range(shards):
        start = shard * part // 128 * 128
        block_ref[shard] = jnp.concatenate(
            [whole] + [total[:, start : start + 128] for total in sums[2:]], axis=1
        )


def mixture(hidden, policy_own, policy_other, reference_own, reference_other, weight, token):
    shards, _, part, width = hidden.shape
    vocab = policy_own.shape[0]
    seqs = shards * part
    chunks = 7
    return pl.pallas_call(
        mixture_kernel,
        in_specs=[HBM, VMEM] + [HBM] * 3 + [VMEM] * 2,
        out_specs=[VMEM] * 3,
        out_shape=[
            jax.ShapeDtypeStruct((seqs, vocab), jnp.float32),
            jax.ShapeDtypeStruct((seqs, vocab), jnp.float32),
            jax.ShapeDtypeStruct((shards, 1, 2 * seqs + 3 * 128), jnp.float32),
        ],
        scratch_shapes=[
            pltpu.VMEM((shards, 2, part, width), jnp.bfloat16),
            pltpu.VMEM((3, vocab, width), jnp.bfloat16),
            pltpu.VMEM((seqs, 2 * vocab), jnp.float32),
            pltpu.VMEM((seqs, 2 * vocab), jnp.float32),
            pltpu.VMEM((5, seqs, 128), jnp.float32),
            pltpu.SemaphoreType.DMA((chunks, 4)),
        ],
        compiler_params=pltpu.CompilerParams(vmem_limit_bytes=32 * MIB),
        name="mixture",
    )(
        in_hbm(hidden),
        pltpu.with_memory_space_constraint(policy_own, pltpu.VMEM),
        in_hbm(policy_other),
        in_hbm(reference_own),
        in_hbm(reference_other),
        weight,
        token,
    )


def finish_kernel(place_ref, own_ref, other_ref, totals_ref, weight_ref, shift_ref, sampled_ref, staged, sem):
    shards, _, part, vocab = shift_ref.shape
    seqs = shards * part
    half = place_ref[0]
    shard = place_ref[1]

    totals = [totals_ref[k] for k in range(2)]
    logs = [jnp.log(total[:, : 2 * seqs + 128]) for total in totals]
    deltas = [log[:, :seqs] - log[:, seqs : 2 * seqs] for log in logs]
    own_first = half == 0
    turns = (
        jnp.where(own_first, deltas[0], deltas[1]),
        jnp.where(own_first, deltas[1], deltas[0]),
    )

    chunk = 128
    per = chunk // part
    stores = []
    for turn, diff_ref in enumerate((own_ref, other_ref)):
        target = half if turn == 0 else 1 - half
        for j in range(seqs // chunk):
            delta = jnp.broadcast_to(turns[turn][:, j * chunk : (j + 1) * chunk], (chunk, chunk)).T
            shards_here = pl.ds(j * per, per)
            for group in range(vocab // 128):
                lanes = pl.ds(group * 128, 128)
                shifted = diff_ref[pl.ds(j * chunk, chunk), lanes] + delta
                staged[turn, shards_here, :, lanes] = shifted.reshape(per, part, 128)
            store = pltpu.make_async_copy(
                staged.at[turn, shards_here],
                shift_ref.at[shards_here, target],
                sem.at[turn, j],
            )
            store.start()
            stores.append(store)

    mine = shard * part // 128
    picked = []
    for total, log in zip(totals, logs):
        policy = jnp.zeros((1, 128), jnp.float32)
        mixed = jnp.zeros((1, 128), jnp.float32)
        for j in range(seqs // 128):
            policy = jnp.where(mine == j, log[:, j * 128 : (j + 1) * 128], policy)
            mixed = jnp.where(mine == j, log[:, seqs + j * 128 : seqs + (j + 1) * 128], mixed)
        policy_pick = total[:, 2 * seqs + 128 : 2 * seqs + 256]
        reference_pick = total[:, 2 * seqs + 256 : 2 * seqs + 384]
        picked.append((policy_pick, reference_pick, policy, log[:, 2 * seqs :], mixed))
    lane = lax.broadcasted_iota(jnp.int32, (8, 128), 1)
    start = shard * part % 128
    values = []
    for low, high in zip(*picked):
        low = pltpu.roll(jnp.broadcast_to(low, (8, 128)), lax.rem(128 - start, 128), 1)
        high = pltpu.roll(jnp.broadcast_to(high, (8, 128)), lax.rem(128 + part - start, 128), 1)
        values.append(jnp.where(lane < part, low, high)[:1, : 2 * part])
    policy_pick, reference_pick, policy_log, reference_log, mixed_log = values
    weight = weight_ref[...]
    sampled_ref[0:1, :] = policy_pick - policy_log
    sampled_ref[1:2, :] = reference_pick - reference_log
    sampled_ref[2:3, :] = (1.0 - weight) * policy_pick + weight * reference_pick - mixed_log

    for store in stores:
        store.wait()


def finish(place, diff_own, diff_other, totals, weight, shards):
    seqs, vocab = diff_own.shape
    part = seqs // shards
    return pl.pallas_call(
        finish_kernel,
        in_specs=[pl.BlockSpec(memory_space=pltpu.SMEM)] + [VMEM] * 4,
        out_specs=[HBM, VMEM],
        out_shape=[
            jax.ShapeDtypeStruct((shards, 2, part, vocab), jnp.float32),
            jax.ShapeDtypeStruct((3, 2 * part), jnp.float32),
        ],
        scratch_shapes=[
            pltpu.VMEM((2, shards, part, vocab), jnp.float32),
            pltpu.SemaphoreType.DMA((2, seqs // 128)),
        ],
        compiler_params=pltpu.CompilerParams(vmem_limit_bytes=16 * MIB),
        name="finish",
    )(place, diff_own, diff_other, totals, weight)


def partners(z, y, x):
    pairs = []
    for source in range(z * 2 * y * x):
        i, rest = divmod(source, 2 * y * x)
        c, rest = divmod(rest, y * x)
        j, k = divmod(rest, x)
        j, k = (j, k ^ 1) if c == 0 else (j ^ 1, k)
        pairs.append((source, ((i * 2 + c) * y + j) * x + k))
    return pairs


def local(
    policy_hidden,
    reference_hidden,
    policy_gain,
    reference_gain,
    policy_embedding,
    reference_embedding,
    mixture_weight,
    sampled_tokens,
):
    seq_local = policy_hidden.shape[0]
    part = seq_local // 2
    vocab = policy_embedding.shape[0]
    shards = lax.axis_size(DP)
    copies = lax.axis_size(MP)
    shard = lax.axis_index(DP)
    copy = lax.axis_index(MP)
    core = lax.axis_index("dp_1")
    row = lax.axis_index("mp_0")
    column = lax.axis_index("mp_1")
    half = (row + column) % 2
    other_copy = jnp.where(
        core == 0,
        row * lax.axis_size("mp_1") + (column ^ 1),
        (row ^ 1) * lax.axis_size("mp_1") + column,
    )
    first_own = (shard * copies + copy) * vocab
    first_other = (shard * copies + other_copy) * vocab
    place = jnp.stack([half, shard]).astype(jnp.int32)
    pairs = partners(lax.axis_size("dp_0"), lax.axis_size("mp_0"), lax.axis_size("mp_1"))

    normed = normalize(place, policy_hidden, reference_hidden, policy_gain, reference_gain)
    normed, policy_send, reference_send = lax.optimization_barrier(
        (normed, policy_embedding, reference_embedding)
    )
    hidden = lax.all_gather(normed, DP, axis=0)
    policy_other = lax.ppermute(policy_send, DP_MP, pairs)
    reference_other = lax.ppermute(reference_send, DP_MP, pairs)

    seqs = shards * part
    weights = mixture_weight.reshape(shards, 2, part)
    tokens = sampled_tokens.reshape(shards, 2, part)
    weight = lax.dynamic_index_in_dim(weights, half, 1, False).reshape(seqs, 1)
    token = lax.dynamic_index_in_dim(tokens, half, 1, False).reshape(seqs, 1)
    token = jnp.stack([token - first_own, token - first_other])
    weight = jnp.broadcast_to(weight, (seqs, 128))
    token = jnp.broadcast_to(token, (2, seqs, 128))
    weight_mine = lax.dynamic_slice_in_dim(mixture_weight, shard * seq_local, seq_local)[None]
    policy_other, reference_other, weight, token = lax.optimization_barrier(
        (policy_other, reference_other, weight, token)
    )
    diff_own, diff_send, block = mixture(
        hidden, policy_embedding, policy_other, reference_embedding, reference_other, weight, token
    )

    block = lax.all_to_all(block, DP, 0, 0, tiled=True)
    diff_other = lax.ppermute(diff_send, DP_MP, pairs)
    block = jnp.sum(block, axis=0, keepdims=True)
    block = jnp.broadcast_to(block, (copies,) + block.shape[1:])
    blocks = lax.all_to_all(block, MP, 0, 0, tiled=True)
    index = lax.broadcasted_iota(jnp.int32, (copies, 1, 1), 0)
    columns = lax.axis_size("mp_1")
    odd = (index // columns + index % columns) % 2 == 1
    totals = jnp.stack(
        [jnp.sum(jnp.where(odd, 0.0, blocks), axis=0), jnp.sum(jnp.where(odd, blocks, 0.0), axis=0)]
    )
    mixture_shift, sampled_logprobs = finish(
        place, diff_own, diff_other, totals, weight_mine, shards
    )
    return (mixture_shift.reshape(shards * seq_local, vocab), sampled_logprobs)


def solution(mesh):
    split = Mesh(mesh.devices.reshape(8, 2, 8, 4), ("dp_0", "dp_1", "mp_0", "mp_1"))
    in_specs = (P(DP, None), P(DP, None), P(), P(), P(DP_MP, None), P(DP_MP, None), P(), P())
    out_specs = (P(None, DP_MP), P(None, DP))
    return jax.shard_map(local, mesh=split, in_specs=in_specs, out_specs=out_specs, check_vma=False)
```

```python
import functools

import jax
import jax.numpy as jnp
from jax import lax
from jax.experimental import pallas as pl
from jax.experimental.pallas import tpu as pltpu
from jax.sharding import Mesh
from jax.sharding import PartitionSpec as P

DP = ("dp_0", "dp_1")
MP = ("mp_0", "mp_1")
DP_MP = ("dp_0", "dp_1", "mp_0", "mp_1")

softcap = 30.0
epsilon = 1e-06

MIB = 1024 * 1024
HBM = pl.BlockSpec(memory_space=pltpu.HBM)
VMEM = pl.BlockSpec(memory_space=pltpu.VMEM)


def in_hbm(x):
    return pltpu.with_memory_space_constraint(x, pltpu.HBM)


def normalize_kernel(half_ref, policy_ref, reference_ref, policy_gain_ref, reference_gain_ref, out_ref, rows, in_sem):
    part = out_ref.shape[1]
    first = pl.multiple_of(half_ref[0] * part, part)
    models = ((policy_ref, policy_gain_ref), (reference_ref, reference_gain_ref))
    loads = [
        pltpu.make_async_copy(hidden_ref.at[pl.ds(first, part), :], rows.at[model], in_sem.at[model])
        for model, (hidden_ref, _) in enumerate(models)
    ]
    for load in loads:
        load.start()
    for model, (_, gain_ref) in enumerate(models):
        loads[model].wait()
        values = rows[model].astype(jnp.float32)
        meansq = jnp.mean(values * values, axis=-1, keepdims=True)
        gain = gain_ref[...].reshape(1, values.shape[1])
        normed = values * lax.rsqrt(meansq + epsilon) * gain
        out_ref[model] = normed.astype(jnp.bfloat16)


def normalize(half, policy_hidden, reference_hidden, policy_gain, reference_gain):
    rows, width = policy_hidden.shape
    part = rows // 2
    return pl.pallas_call(
        normalize_kernel,
        in_specs=[pl.BlockSpec(memory_space=pltpu.SMEM)] + [HBM] * 2 + [VMEM] * 2,
        out_specs=VMEM,
        out_shape=jax.ShapeDtypeStruct((2, part, width), jnp.bfloat16),
        scratch_shapes=[pltpu.VMEM((2, part, width), jnp.bfloat16), pltpu.SemaphoreType.DMA((2,))],
        compiler_params=pltpu.CompilerParams(vmem_limit_bytes=16 * MIB),
        name="normalize",
    )(half, in_hbm(policy_hidden), in_hbm(reference_hidden), in_hbm(policy_gain), in_hbm(reference_gain))


def mixture_kernel(
    hidden_ref,
    policy_own_ref,
    policy_other_ref,
    reference_own_ref,
    reference_other_ref,
    weight_ref,
    token_ref,
    diff_own_ref,
    diff_other_ref,
    block_ref,
    hidden,
    loaded,
    policy_acc,
    reference_acc,
    partial,
    sem,
):
    chunks = sem.shape[0]
    shards, _, part, width = hidden_ref.shape
    depth = width // chunks
    vocab = policy_own_ref.shape[0]
    seqs = shards * part

    def loads(k):
        columns = pl.ds(k * depth, depth)
        rest = (policy_other_ref, reference_own_ref, reference_other_ref)
        pairs = [(hidden_ref.at[:, :, :, columns], hidden.at[:, :, :, columns])]
        pairs += [(ref.at[:, columns], loaded.at[i, :, columns]) for i, ref in enumerate(rest)]
        return [pltpu.make_async_copy(*pair, sem.at[k, i]) for i, pair in enumerate(pairs)]

    for k in range(chunks):
        for load in loads(k):
            load.start()
    for k in range(chunks):
        for load in loads(k):
            load.wait()
        columns = pl.ds(k * depth, depth)
        for model, acc in enumerate((policy_acc, reference_acc)):
            left = hidden[:, model, :, columns].reshape(seqs, depth)
            for place in range(2):
                index = 2 * model + place
                rows = policy_own_ref[:, columns] if index == 0 else loaded[index - 1, :, columns]
                product = lax.dot_general(
                    left, rows, (((1,), (1,)), ((), ())), preferred_element_type=jnp.float32
                )
                target = pl.ds(place * vocab, vocab)
                acc[:, target] = product if k == 0 else acc[:, target] + product

    def body(i, carry):
        rows = pl.ds(pl.multiple_of(i * 8, 8), 8)
        weight = weight_ref[rows, :]
        keep = 1.0 - weight
        sums = [jnp.zeros((8, 128), jnp.float32) for _ in range(5)]
        for place, diff_ref in enumerate((diff_own_ref, diff_other_ref)):
            token = token_ref[place, rows, :]
            for group in range(vocab // 128):
                lanes = pl.ds(place * vocab + group * 128, 128)
                policy = softcap * jnp.tanh(policy_acc[rows, lanes] * (1.0 / softcap))
                reference = softcap * jnp.tanh(reference_acc[rows, lanes] * (1.0 / softcap))
                mixed = keep * policy + weight * reference
                diff_ref[rows, pl.ds(group * 128, 128)] = mixed - policy
                hit = lax.broadcasted_iota(jnp.int32, (8, 128), 1) + group * 128 == token
                terms = (
                    jnp.exp(policy),
                    jnp.exp(mixed),
                    jnp.exp(reference),
                    jnp.where(hit, policy, 0.0),
                    jnp.where(hit, reference, 0.0),
                )
                sums = [total + term for total, term in zip(sums, terms)]
        for k in range(5):
            partial[k, rows, :] = sums[k]
        return carry

    lax.fori_loop(0, seqs // 8, body, 0, unroll=8)
    sums = [jnp.sum(partial[k].T, axis=0, keepdims=True) for k in range(5)]
    whole = jnp.concatenate(sums[:2], axis=1)
    for shard in range(shards):
        start = shard * part // 128 * 128
        block_ref[shard] = jnp.concatenate(
            [whole] + [total[:, start : start + 128] for total in sums[2:]], axis=1
        )


def mixture(hidden, policy_own, policy_other, reference_own, reference_other, weight, token):
    shards, _, part, width = hidden.shape
    vocab = policy_own.shape[0]
    seqs = shards * part
    chunks = 7
    return pl.pallas_call(
        mixture_kernel,
        in_specs=[HBM, VMEM] + [HBM] * 3 + [VMEM] * 2,
        out_specs=[VMEM] * 3,
        out_shape=[
            jax.ShapeDtypeStruct((seqs, vocab), jnp.float32),
            jax.ShapeDtypeStruct((seqs, vocab), jnp.float32),
            jax.ShapeDtypeStruct((shards, 1, 2 * seqs + 3 * 128), jnp.float32),
        ],
        scratch_shapes=[
            pltpu.VMEM((shards, 2, part, width), jnp.bfloat16),
            pltpu.VMEM((3, vocab, width), jnp.bfloat16),
            pltpu.VMEM((seqs, 2 * vocab), jnp.float32),
            pltpu.VMEM((seqs, 2 * vocab), jnp.float32),
            pltpu.VMEM((5, seqs, 128), jnp.float32),
            pltpu.SemaphoreType.DMA((chunks, 4)),
        ],
        compiler_params=pltpu.CompilerParams(vmem_limit_bytes=32 * MIB),
        name="mixture",
    )(
        in_hbm(hidden),
        pltpu.with_memory_space_constraint(policy_own, pltpu.VMEM),
        in_hbm(policy_other),
        in_hbm(reference_own),
        in_hbm(reference_other),
        weight,
        token,
    )


def finish_kernel(place_ref, own_ref, other_ref, totals_ref, blocks_ref, weight_ref, shift_ref, sampled_ref, staged, sem):
    shards, _, part, vocab = shift_ref.shape
    seqs = shards * part
    half = place_ref[0]
    shard = place_ref[1]

    totals = [totals_ref[k] for k in range(2)]
    logs = [jnp.log(total[:, : 2 * seqs + 128]) for total in totals]
    deltas = [log[:, :seqs] - log[:, seqs : 2 * seqs] for log in logs]
    own_first = half == 0
    partner = blocks_ref[place_ref[2]]
    center = jnp.log(partner[:, :seqs]) - jnp.log(partner[:, seqs : 2 * seqs])
    turns = (
        jnp.where(own_first, deltas[0], deltas[1]),
        jnp.where(own_first, deltas[1], deltas[0]) - center,
    )

    chunk = 128
    per = chunk // part
    stores = []
    for turn, diff_ref in enumerate((own_ref, other_ref)):
        target = half if turn == 0 else 1 - half
        for j in range(seqs // chunk):
            delta = jnp.broadcast_to(turns[turn][:, j * chunk : (j + 1) * chunk], (chunk, chunk)).T
            shards_here = pl.ds(j * per, per)
            for group in range(vocab // 128):
                lanes = pl.ds(group * 128, 128)
                shifted = diff_ref[pl.ds(j * chunk, chunk), lanes].astype(jnp.float32) + delta
                staged[turn, shards_here, :, lanes] = shifted.reshape(per, part, 128)
            store = pltpu.make_async_copy(
                staged.at[turn, shards_here],
                shift_ref.at[shards_here, target],
                sem.at[turn, j],
            )
            store.start()
            stores.append(store)

    mine = shard * part // 128
    picked = []
    for total, log in zip(totals, logs):
        policy = jnp.zeros((1, 128), jnp.float32)
        mixed = jnp.zeros((1, 128), jnp.float32)
        for j in range(seqs // 128):
            policy = jnp.where(mine == j, log[:, j * 128 : (j + 1) * 128], policy)
            mixed = jnp.where(mine == j, log[:, seqs + j * 128 : seqs + (j + 1) * 128], mixed)
        policy_pick = total[:, 2 * seqs + 128 : 2 * seqs + 256]
        reference_pick = total[:, 2 * seqs + 256 : 2 * seqs + 384]
        picked.append((policy_pick, reference_pick, policy, log[:, 2 * seqs :], mixed))
    lane = lax.broadcasted_iota(jnp.int32, (8, 128), 1)
    start = shard * part % 128
    values = []
    for low, high in zip(*picked):
        low = pltpu.roll(jnp.broadcast_to(low, (8, 128)), lax.rem(128 - start, 128), 1)
        high = pltpu.roll(jnp.broadcast_to(high, (8, 128)), lax.rem(128 + part - start, 128), 1)
        values.append(jnp.where(lane < part, low, high)[:1, : 2 * part])
    policy_pick, reference_pick, policy_log, reference_log, mixed_log = values
    weight = weight_ref[...]
    sampled_ref[0:1, :] = policy_pick - policy_log
    sampled_ref[1:2, :] = reference_pick - reference_log
    sampled_ref[2:3, :] = (1.0 - weight) * policy_pick + weight * reference_pick - mixed_log

    for store in stores:
        store.wait()


def finish(place, diff_own, diff_other, totals, blocks, weight, shards):
    seqs, vocab = diff_own.shape
    part = seqs // shards
    return pl.pallas_call(
        finish_kernel,
        in_specs=[pl.BlockSpec(memory_space=pltpu.SMEM)] + [VMEM] * 5,
        out_specs=[HBM, VMEM],
        out_shape=[
            jax.ShapeDtypeStruct((shards, 2, part, vocab), jnp.float32),
            jax.ShapeDtypeStruct((3, 2 * part), jnp.float32),
        ],
        scratch_shapes=[
            pltpu.VMEM((2, shards, part, vocab), jnp.float32),
            pltpu.SemaphoreType.DMA((2, seqs // 128)),
        ],
        compiler_params=pltpu.CompilerParams(vmem_limit_bytes=16 * MIB),
        name="finish",
    )(place, diff_own, diff_other, totals, blocks, weight)


def partners(z, y, x):
    pairs = []
    for source in range(z * 2 * y * x):
        i, rest = divmod(source, 2 * y * x)
        c, rest = divmod(rest, y * x)
        j, k = divmod(rest, x)
        j, k = (j, k ^ 1) if c == 0 else (j ^ 1, k)
        pairs.append((source, ((i * 2 + c) * y + j) * x + k))
    return pairs


def local(
    policy_hidden,
    reference_hidden,
    policy_gain,
    reference_gain,
    policy_embedding,
    reference_embedding,
    mixture_weight,
    sampled_tokens,
):
    seq_local = policy_hidden.shape[0]
    part = seq_local // 2
    vocab = policy_embedding.shape[0]
    shards = lax.axis_size(DP)
    copies = lax.axis_size(MP)
    shard = lax.axis_index(DP)
    copy = lax.axis_index(MP)
    core = lax.axis_index("dp_1")
    row = lax.axis_index("mp_0")
    column = lax.axis_index("mp_1")
    half = (row + column) % 2
    other_copy = jnp.where(
        core == 0,
        row * lax.axis_size("mp_1") + (column ^ 1),
        (row ^ 1) * lax.axis_size("mp_1") + column,
    )
    first_own = (shard * copies + copy) * vocab
    first_other = (shard * copies + other_copy) * vocab
    place = jnp.stack([half, shard, other_copy]).astype(jnp.int32)
    pairs = partners(lax.axis_size("dp_0"), lax.axis_size("mp_0"), lax.axis_size("mp_1"))

    normed = normalize(place, policy_hidden, reference_hidden, policy_gain, reference_gain)
    normed, policy_send, reference_send = lax.optimization_barrier(
        (normed, policy_embedding, reference_embedding)
    )
    hidden = lax.all_gather(normed, DP, axis=0)
    policy_other = lax.ppermute(policy_send, DP_MP, pairs)
    reference_other = lax.ppermute(reference_send, DP_MP, pairs)

    seqs = shards * part
    weights = mixture_weight.reshape(shards, 2, part)
    tokens = sampled_tokens.reshape(shards, 2, part)
    weight = lax.dynamic_index_in_dim(weights, half, 1, False).reshape(seqs, 1)
    token = lax.dynamic_index_in_dim(tokens, half, 1, False).reshape(seqs, 1)
    token = jnp.stack([token - first_own, token - first_other])
    weight = jnp.broadcast_to(weight, (seqs, 128))
    token = jnp.broadcast_to(token, (2, seqs, 128))
    weight_mine = lax.dynamic_slice_in_dim(mixture_weight, shard * seq_local, seq_local)[None]
    policy_other, reference_other, weight, token = lax.optimization_barrier(
        (policy_other, reference_other, weight, token)
    )
    diff_own, diff_send, block = mixture(
        hidden, policy_embedding, policy_other, reference_embedding, reference_other, weight, token
    )

    block = jnp.sum(lax.all_to_all(block, DP, 0, 0, tiled=True), axis=0, keepdims=True)
    center = jnp.log(block[0, 0, :seqs]) - jnp.log(block[0, 0, seqs : 2 * seqs])
    diff_send = (diff_send + center[:, None]).astype(jnp.bfloat16)
    diff_other = lax.ppermute(diff_send, DP_MP, pairs)
    block = jnp.broadcast_to(block, (copies,) + block.shape[1:])
    blocks = lax.all_to_all(block, MP, 0, 0, tiled=True)
    index = lax.broadcasted_iota(jnp.int32, (copies, 1, 1), 0)
    columns = lax.axis_size("mp_1")
    odd = (index // columns + index % columns) % 2 == 1
    totals = jnp.stack(
        [jnp.sum(jnp.where(odd, 0.0, blocks), axis=0), jnp.sum(jnp.where(odd, blocks, 0.0), axis=0)]
    )
    mixture_shift, sampled_logprobs = finish(
        place, diff_own, diff_other, totals, blocks, weight_mine, shards
    )
    return (mixture_shift.reshape(shards * seq_local, vocab), sampled_logprobs)


def solution(mesh):
    split = Mesh(mesh.devices.reshape(8, 2, 8, 4), ("dp_0", "dp_1", "mp_0", "mp_1"))
    in_specs = (P(DP, None), P(DP, None), P(), P(), P(DP_MP, None), P(DP_MP, None), P(), P())
    out_specs = (P(None, DP_MP), P(None, DP))
    return jax.shard_map(local, mesh=split, in_specs=in_specs, out_specs=out_specs, check_vma=False)
```

```python
import functools

import jax
import jax.numpy as jnp
from jax import lax
from jax.experimental import pallas as pl
from jax.experimental.pallas import tpu as pltpu
from jax.sharding import Mesh
from jax.sharding import PartitionSpec as P

DP = ("dp_0", "dp_1")
MP = ("mp_0", "mp_1")
DP_MP = ("dp_0", "dp_1", "mp_0", "mp_1")

softcap = 30.0
epsilon = 1e-06

MIB = 1024 * 1024
HBM = pl.BlockSpec(memory_space=pltpu.HBM)
VMEM = pl.BlockSpec(memory_space=pltpu.VMEM)


def in_hbm(x):
    return pltpu.with_memory_space_constraint(x, pltpu.HBM)


def normalize_kernel(
    place_ref, policy_ref, reference_ref, policy_gain_ref, reference_gain_ref, main_ref, quarter_ref, rows, in_sem
):
    part, width = rows.shape[1:]
    depth = width // 4
    first = pl.multiple_of(place_ref[0] * part, part)
    models = ((policy_ref, policy_gain_ref), (reference_ref, reference_gain_ref))
    loads = [
        pltpu.make_async_copy(hidden_ref.at[pl.ds(first, part), :], rows.at[model], in_sem.at[model])
        for model, (hidden_ref, _) in enumerate(models)
    ]
    for load in loads:
        load.start()
    for model, (_, gain_ref) in enumerate(models):
        loads[model].wait()
        values = rows[model].astype(jnp.float32)
        meansq = jnp.mean(values * values, axis=-1, keepdims=True)
        gain = gain_ref[...].reshape(1, width)
        normed = (values * lax.rsqrt(meansq + epsilon) * gain).astype(jnp.bfloat16)
        if model == 0:
            main_ref[: part // 2] = normed[: part // 2]
            for i in range(4):

                @pl.when(place_ref[2] == i)
                def _(i=i, normed=normed):
                    quarter_ref[...] = normed[part // 2 :, i * depth : (i + 1) * depth]
        else:
            main_ref[part // 2 :] = normed


def normalize(place, policy_hidden, reference_hidden, policy_gain, reference_gain):
    rows, width = policy_hidden.shape
    part = rows // 2
    return pl.pallas_call(
        normalize_kernel,
        in_specs=[pl.BlockSpec(memory_space=pltpu.SMEM)] + [HBM] * 2 + [VMEM] * 2,
        out_specs=[VMEM] * 2,
        out_shape=[
            jax.ShapeDtypeStruct((part + part // 2, width), jnp.bfloat16),
            jax.ShapeDtypeStruct((part // 2, width // 4), jnp.bfloat16),
        ],
        scratch_shapes=[pltpu.VMEM((2, part, width), jnp.bfloat16), pltpu.SemaphoreType.DMA((2,))],
        compiler_params=pltpu.CompilerParams(vmem_limit_bytes=16 * MIB),
        name="normalize",
    )(place, in_hbm(policy_hidden), in_hbm(reference_hidden), in_hbm(policy_gain), in_hbm(reference_gain))


def mixture_kernel(
    place_ref,
    main_ref,
    quarter_0_ref,
    quarter_1_ref,
    quarter_2_ref,
    quarter_3_ref,
    policy_own_ref,
    policy_other_ref,
    reference_own_ref,
    reference_other_ref,
    weight_ref,
    token_ref,
    diff_own_ref,
    diff_other_ref,
    block_ref,
    hidden,
    loaded,
    policy_acc,
    reference_acc,
    partial,
    sem,
    quarter_sem,
):
    chunks = sem.shape[0]
    shards, _, part, width = hidden.shape
    depth = width // chunks
    vocab = policy_own_ref.shape[0]
    seqs = shards * part

    def loads(k):
        columns = pl.ds(k * depth, depth)
        low = pl.ds(0, part // 2)
        rest = (policy_other_ref, reference_own_ref, reference_other_ref)
        pairs = [
            (main_ref.at[:, low, columns], hidden.at[:, 0, low, columns]),
            (main_ref.at[:, pl.ds(part // 2, part), columns], hidden.at[:, 1, :, columns]),
        ]
        pairs += [(ref.at[:, columns], loaded.at[i, :, columns]) for i, ref in enumerate(rest)]
        return [pltpu.make_async_copy(*pair, sem.at[k, i]) for i, pair in enumerate(pairs)]

    quarters = []
    for i, ref in enumerate((quarter_0_ref, quarter_1_ref, quarter_2_ref, quarter_3_ref)):
        start = pl.multiple_of((place_ref[2] ^ i) * (width // 4), 128)
        target = hidden.at[:, 0, pl.ds(part // 2, part // 2), pl.ds(start, width // 4)]
        quarters.append(pltpu.make_async_copy(ref, target, quarter_sem.at[i]))
    for quarter in quarters:
        quarter.start()
    for k in range(chunks):
        for load in loads(k):
            load.start()
    for quarter in quarters:
        quarter.wait()
    for k in range(chunks):
        for load in loads(k):
            load.wait()
        columns = pl.ds(k * depth, depth)
        for model, acc in enumerate((policy_acc, reference_acc)):
            left = hidden[:, model, :, columns].reshape(seqs, depth)
            for place in range(2):
                index = 2 * model + place
                rows = policy_own_ref[:, columns] if index == 0 else loaded[index - 1, :, columns]
                product = lax.dot_general(
                    left, rows, (((1,), (1,)), ((), ())), preferred_element_type=jnp.float32
                )
                target = pl.ds(place * vocab, vocab)
                acc[:, target] = product if k == 0 else acc[:, target] + product

    def body(i, carry):
        rows = pl.ds(pl.multiple_of(i * 8, 8), 8)
        weight = weight_ref[rows, :]
        keep = 1.0 - weight
        sums = [jnp.zeros((8, 128), jnp.float32) for _ in range(5)]
        for place, diff_ref in enumerate((diff_own_ref, diff_other_ref)):
            token = token_ref[place, rows, :]
            for group in range(vocab // 128):
                lanes = pl.ds(place * vocab + group * 128, 128)
                policy = softcap * jnp.tanh(policy_acc[rows, lanes] * (1.0 / softcap))
                reference = softcap * jnp.tanh(reference_acc[rows, lanes] * (1.0 / softcap))
                mixed = keep * policy + weight * reference
                diff_ref[rows, pl.ds(group * 128, 128)] = mixed - policy
                hit = lax.broadcasted_iota(jnp.int32, (8, 128), 1) + group * 128 == token
                terms = (
                    jnp.exp(policy),
                    jnp.exp(mixed),
                    jnp.exp(reference),
                    jnp.where(hit, policy, 0.0),
                    jnp.where(hit, reference, 0.0),
                )
                sums = [total + term for total, term in zip(sums, terms)]
        for k in range(5):
            partial[k, rows, :] = sums[k]
        return carry

    lax.fori_loop(0, seqs // 8, body, 0, unroll=8)
    sums = [jnp.sum(partial[k].T, axis=0, keepdims=True) for k in range(5)]
    whole = jnp.concatenate(sums[:2], axis=1)
    for shard in range(shards):
        start = shard * part // 128 * 128
        block_ref[shard] = jnp.concatenate(
            [whole] + [total[:, start : start + 128] for total in sums[2:]], axis=1
        )


def mixture(place, main, quarters, policy_own, policy_other, reference_own, reference_other, weight, token):
    shards, rows, width = main.shape
    part = rows // 3 * 2
    vocab = policy_own.shape[0]
    seqs = shards * part
    chunks = 7
    return pl.pallas_call(
        mixture_kernel,
        in_specs=[pl.BlockSpec(memory_space=pltpu.SMEM)] + [HBM] * 5 + [VMEM] + [HBM] * 3 + [VMEM] * 2,
        out_specs=[VMEM] * 3,
        out_shape=[
            jax.ShapeDtypeStruct((seqs, vocab), jnp.float32),
            jax.ShapeDtypeStruct((seqs, vocab), jnp.float32),
            jax.ShapeDtypeStruct((shards, 1, 2 * seqs + 3 * 128), jnp.float32),
        ],
        scratch_shapes=[
            pltpu.VMEM((shards, 2, part, width), jnp.bfloat16),
            pltpu.VMEM((3, vocab, width), jnp.bfloat16),
            pltpu.VMEM((seqs, 2 * vocab), jnp.float32),
            pltpu.VMEM((seqs, 2 * vocab), jnp.float32),
            pltpu.VMEM((5, seqs, 128), jnp.float32),
            pltpu.SemaphoreType.DMA((chunks, 5)),
            pltpu.SemaphoreType.DMA((4,)),
        ],
        compiler_params=pltpu.CompilerParams(vmem_limit_bytes=32 * MIB),
        name="mixture",
    )(
        place,
        in_hbm(main),
        *map(in_hbm, quarters),
        pltpu.with_memory_space_constraint(policy_own, pltpu.VMEM),
        in_hbm(policy_other),
        in_hbm(reference_own),
        in_hbm(reference_other),
        weight,
        token,
    )


def finish_kernel(columns, place_ref, own_ref, other_ref, blocks_ref, weight_ref, shift_ref, sampled_ref, staged, sem):
    shards, _, part, vocab = shift_ref.shape
    seqs = shards * part
    half = place_ref[0]
    shard = place_ref[1]

    totals = [None, None]
    for j in range(blocks_ref.shape[0]):
        k = half_bit(j // columns, j % columns)
        totals[k] = blocks_ref[j] if totals[k] is None else totals[k] + blocks_ref[j]
    logs = [jnp.log(total[:, : 2 * seqs + 128]) for total in totals]
    deltas = [log[:, :seqs] - log[:, seqs : 2 * seqs] for log in logs]
    own_first = half == 0
    turns = (
        jnp.where(own_first, deltas[0], deltas[1]),
        jnp.where(own_first, deltas[1], deltas[0]),
    )

    chunk = 128
    per = chunk // part
    stores = []
    for turn, diff_ref in enumerate((own_ref, other_ref)):
        target = half if turn == 0 else 1 - half
        for j in range(seqs // chunk):
            delta = jnp.broadcast_to(turns[turn][:, j * chunk : (j + 1) * chunk], (chunk, chunk)).T
            shards_here = pl.ds(j * per, per)
            for group in range(vocab // 128):
                lanes = pl.ds(group * 128, 128)
                shifted = diff_ref[pl.ds(j * chunk, chunk), lanes] + delta
                staged[turn, shards_here, :, lanes] = shifted.reshape(per, part, 128)
            store = pltpu.make_async_copy(
                staged.at[turn, shards_here],
                shift_ref.at[shards_here, target],
                sem.at[turn, j],
            )
            store.start()
            stores.append(store)

    mine = shard * part // 128
    picked = []
    for total, log in zip(totals, logs):
        policy = jnp.zeros((1, 128), jnp.float32)
        mixed = jnp.zeros((1, 128), jnp.float32)
        for j in range(seqs // 128):
            policy = jnp.where(mine == j, log[:, j * 128 : (j + 1) * 128], policy)
            mixed = jnp.where(mine == j, log[:, seqs + j * 128 : seqs + (j + 1) * 128], mixed)
        policy_pick = total[:, 2 * seqs + 128 : 2 * seqs + 256]
        reference_pick = total[:, 2 * seqs + 256 : 2 * seqs + 384]
        picked.append((policy_pick, reference_pick, policy, log[:, 2 * seqs :], mixed))
    lane = lax.broadcasted_iota(jnp.int32, (8, 128), 1)
    start = shard * part % 128
    values = []
    for low, high in zip(*picked):
        low = pltpu.roll(jnp.broadcast_to(low, (8, 128)), lax.rem(128 - start, 128), 1)
        high = pltpu.roll(jnp.broadcast_to(high, (8, 128)), lax.rem(128 + part - start, 128), 1)
        values.append(jnp.where(lane < part, low, high)[:1, : 2 * part])
    policy_pick, reference_pick, policy_log, reference_log, mixed_log = values
    weight = weight_ref[...]
    sampled_ref[0:1, :] = policy_pick - policy_log
    sampled_ref[1:2, :] = reference_pick - reference_log
    sampled_ref[2:3, :] = (1.0 - weight) * policy_pick + weight * reference_pick - mixed_log

    for store in stores:
        store.wait()


def finish(place, columns, diff_own, diff_other, blocks, weight, shards):
    seqs, vocab = diff_own.shape
    part = seqs // shards
    return pl.pallas_call(
        functools.partial(finish_kernel, columns),
        in_specs=[pl.BlockSpec(memory_space=pltpu.SMEM)] + [VMEM] * 4,
        out_specs=[HBM, VMEM],
        out_shape=[
            jax.ShapeDtypeStruct((shards, 2, part, vocab), jnp.float32),
            jax.ShapeDtypeStruct((3, 2 * part), jnp.float32),
        ],
        scratch_shapes=[
            pltpu.VMEM((2, shards, part, vocab), jnp.float32),
            pltpu.SemaphoreType.DMA((2, seqs // 128)),
        ],
        compiler_params=pltpu.CompilerParams(vmem_limit_bytes=16 * MIB),
        name="finish",
    )(place, diff_own, diff_other, blocks, weight)


def half_bit(row, column):
    return ((row + 1) // 2 + (column + 1) // 2) % 2


def beside(i, size):
    return (i + 1) % size if i % 2 else (i - 1) % size


def pairs_of(sizes, target):
    z, y, x = sizes
    pairs = []
    for source in range(z * 2 * y * x):
        i, rest = divmod(source, 2 * y * x)
        c, rest = divmod(rest, y * x)
        j, k = target(c, *divmod(rest, x))
        pairs.append((source, ((i * 2 + c) * y + j) * x + k))
    return pairs


def local(
    policy_hidden,
    reference_hidden,
    policy_gain,
    reference_gain,
    policy_embedding,
    reference_embedding,
    mixture_weight,
    sampled_tokens,
):
    seq_local = policy_hidden.shape[0]
    part = seq_local // 2
    vocab = policy_embedding.shape[0]
    shards = lax.axis_size(DP)
    copies = lax.axis_size(MP)
    shard = lax.axis_index(DP)
    copy = lax.axis_index(MP)
    core = lax.axis_index("dp_1")
    row = lax.axis_index("mp_0")
    column = lax.axis_index("mp_1")
    half = half_bit(row, column)
    quarter = 3 - 2 * (row % 2) - column % 2
    other_copy = jnp.where(
        core == 0,
        row * lax.axis_size("mp_1") + (column ^ 1),
        (row ^ 1) * lax.axis_size("mp_1") + column,
    )
    first_own = (shard * copies + copy) * vocab
    first_other = (shard * copies + other_copy) * vocab
    place = jnp.stack([half, shard, quarter]).astype(jnp.int32)
    sizes = lax.axis_size("dp_0"), lax.axis_size("mp_0"), lax.axis_size("mp_1")
    pairs = pairs_of(sizes, lambda c, j, k: (j, k ^ 1) if c == 0 else (j ^ 1, k))
    across = pairs_of(sizes, lambda c, j, k: (j, beside(k, sizes[2])))
    along = pairs_of(sizes, lambda c, j, k: (beside(j, sizes[1]), k))
    aslant = pairs_of(sizes, lambda c, j, k: (beside(j, sizes[1]), beside(k, sizes[2])))

    main, part_quarter = normalize(place, policy_hidden, reference_hidden, policy_gain, reference_gain)
    main, part_quarter, policy_send, reference_send = lax.optimization_barrier(
        (main, part_quarter, policy_embedding, reference_embedding)
    )
    main = lax.all_gather(main, DP, axis=0)
    policy_other = lax.ppermute(policy_send, DP_MP, pairs)
    reference_other = lax.ppermute(reference_send, DP_MP, pairs)
    held = lax.all_gather(part_quarter, DP, axis=0)
    quarters = [held] + [lax.ppermute(held, DP_MP, way) for way in (across, along, aslant)]

    seqs = shards * part
    weights = mixture_weight.reshape(shards, 2, part)
    tokens = sampled_tokens.reshape(shards, 2, part)
    weight = lax.dynamic_index_in_dim(weights, half, 1, False).reshape(seqs, 1)
    token = lax.dynamic_index_in_dim(tokens, half, 1, False).reshape(seqs, 1)
    token = jnp.stack([token - first_own, token - first_other])
    weight = jnp.broadcast_to(weight, (seqs, 128))
    token = jnp.broadcast_to(token, (2, seqs, 128))
    weight_mine = lax.dynamic_slice_in_dim(mixture_weight, shard * seq_local, seq_local)[None]
    policy_other, reference_other, weight, token = lax.optimization_barrier(
        (policy_other, reference_other, weight, token)
    )
    diff_own, diff_send, block = mixture(
        place, main, quarters, policy_embedding, policy_other, reference_embedding, reference_other, weight, token
    )

    block = lax.all_to_all(block, DP, 0, 0, tiled=True)
    block, diff_send = lax.optimization_barrier((block, diff_send))
    diff_other = lax.ppermute(diff_send, DP_MP, pairs)
    block = jnp.sum(block, axis=0, keepdims=True)
    block = jnp.broadcast_to(block, (copies,) + block.shape[1:])
    blocks = lax.all_to_all(block, MP, 0, 0, tiled=True)
    mixture_shift, sampled_logprobs = finish(
        place, lax.axis_size("mp_1"), diff_own, diff_other, blocks, weight_mine, shards
    )
    return (mixture_shift.reshape(shards * seq_local, vocab), sampled_logprobs)


def solution(mesh):
    split = Mesh(mesh.devices.reshape(8, 2, 8, 4), ("dp_0", "dp_1", "mp_0", "mp_1"))
    in_specs = (P(DP, None), P(DP, None), P(), P(), P(DP_MP, None), P(DP_MP, None), P(), P())
    out_specs = (P(None, DP_MP), P(None, DP))
    return jax.shard_map(local, mesh=split, in_specs=in_specs, out_specs=out_specs, check_vma=False)
```

```python
import functools

import jax
import jax.numpy as jnp
from jax import lax
from jax.experimental import pallas as pl
from jax.experimental.pallas import tpu as pltpu
from jax.sharding import Mesh
from jax.sharding import PartitionSpec as P

DP = ("dp_0", "dp_1")
MP = ("mp_0", "mp_1")
DP_MP = ("dp_0", "dp_1", "mp_0", "mp_1")

softcap = 30.0
epsilon = 1e-06

MIB = 1024 * 1024
HBM = pl.BlockSpec(memory_space=pltpu.HBM)
VMEM = pl.BlockSpec(memory_space=pltpu.VMEM)


def in_hbm(x):
    return pltpu.with_memory_space_constraint(x, pltpu.HBM)


def normalize_kernel(
    place_ref, policy_ref, reference_ref, policy_gain_ref, reference_gain_ref, main_ref, quarter_ref, rows, in_sem
):
    part, width = rows.shape[1:]
    depth = width // 4
    first = pl.multiple_of(place_ref[0] * part, part)
    models = ((policy_ref, policy_gain_ref), (reference_ref, reference_gain_ref))
    loads = [
        pltpu.make_async_copy(hidden_ref.at[pl.ds(first, part), :], rows.at[model], in_sem.at[model])
        for model, (hidden_ref, _) in enumerate(models)
    ]
    for load in loads:
        load.start()
    for model, (_, gain_ref) in enumerate(models):
        loads[model].wait()
        values = rows[model].astype(jnp.float32)
        meansq = jnp.mean(values * values, axis=-1, keepdims=True)
        gain = gain_ref[...].reshape(1, width)
        normed = (values * lax.rsqrt(meansq + epsilon) * gain).astype(jnp.bfloat16)
        if model == 0:
            main_ref[: part // 2] = normed[: part // 2]
            for i in range(4):

                @pl.when(place_ref[2] == i)
                def _(i=i, normed=normed):
                    quarter_ref[...] = normed[part // 2 :, i * depth : (i + 1) * depth]
        else:
            main_ref[part // 2 :] = normed


def normalize(place, policy_hidden, reference_hidden, policy_gain, reference_gain):
    rows, width = policy_hidden.shape
    part = rows // 2
    return pl.pallas_call(
        normalize_kernel,
        in_specs=[pl.BlockSpec(memory_space=pltpu.SMEM)] + [HBM] * 2 + [VMEM] * 2,
        out_specs=[VMEM] * 2,
        out_shape=[
            jax.ShapeDtypeStruct((part + part // 2, width), jnp.bfloat16),
            jax.ShapeDtypeStruct((part // 2, width // 4), jnp.bfloat16),
        ],
        scratch_shapes=[pltpu.VMEM((2, part, width), jnp.bfloat16), pltpu.SemaphoreType.DMA((2,))],
        compiler_params=pltpu.CompilerParams(vmem_limit_bytes=16 * MIB),
        name="normalize",
    )(place, in_hbm(policy_hidden), in_hbm(reference_hidden), in_hbm(policy_gain), in_hbm(reference_gain))


def mixture_kernel(
    place_ref,
    main_ref,
    quarter_0_ref,
    quarter_1_ref,
    quarter_2_ref,
    quarter_3_ref,
    policy_own_ref,
    policy_other_ref,
    reference_own_ref,
    reference_other_ref,
    weight_ref,
    token_ref,
    diff_own_ref,
    diff_other_ref,
    block_ref,
    hidden,
    loaded,
    policy_acc,
    reference_acc,
    partial,
    sem,
    quarter_sem,
):
    chunks = sem.shape[0]
    shards, _, part, width = hidden.shape
    depth = width // chunks
    vocab = policy_own_ref.shape[0]
    seqs = shards * part

    def loads(k):
        columns = pl.ds(k * depth, depth)
        low = pl.ds(0, part // 2)
        rest = (policy_other_ref, reference_own_ref, reference_other_ref)
        pairs = [
            (main_ref.at[:, low, columns], hidden.at[:, 0, low, columns]),
            (main_ref.at[:, pl.ds(part // 2, part), columns], hidden.at[:, 1, :, columns]),
        ]
        pairs += [(ref.at[:, columns], loaded.at[i, :, columns]) for i, ref in enumerate(rest)]
        return [pltpu.make_async_copy(*pair, sem.at[k, i]) for i, pair in enumerate(pairs)]

    quarters = []
    core = place_ref[1] % 2
    flips = (0, 1 + core, 2 - core, 3)
    for i, ref in enumerate((quarter_0_ref, quarter_1_ref, quarter_2_ref, quarter_3_ref)):
        start = pl.multiple_of((place_ref[2] ^ flips[i]) * (width // 4), 128)
        target = hidden.at[:, 0, pl.ds(part // 2, part // 2), pl.ds(start, width // 4)]
        quarters.append(pltpu.make_async_copy(ref, target, quarter_sem.at[i]))
    for quarter in quarters:
        quarter.start()
    for k in range(chunks):
        for load in loads(k):
            load.start()
    for quarter in quarters:
        quarter.wait()
    for k in range(chunks):
        for load in loads(k):
            load.wait()
        columns = pl.ds(k * depth, depth)
        for model, acc in enumerate((policy_acc, reference_acc)):
            left = hidden[:, model, :, columns].reshape(seqs, depth)
            for place in range(2):
                index = 2 * model + place
                rows = policy_own_ref[:, columns] if index == 0 else loaded[index - 1, :, columns]
                product = lax.dot_general(
                    left, rows, (((1,), (1,)), ((), ())), preferred_element_type=jnp.float32
                )
                target = pl.ds(place * vocab, vocab)
                acc[:, target] = product if k == 0 else acc[:, target] + product

    def body(i, carry):
        rows = pl.ds(pl.multiple_of(i * 8, 8), 8)
        weight = weight_ref[rows, :]
        keep = 1.0 - weight
        sums = [jnp.zeros((8, 128), jnp.float32) for _ in range(5)]
        for place, diff_ref in enumerate((diff_own_ref, diff_other_ref)):
            token = token_ref[place, rows, :]
            for group in range(vocab // 128):
                lanes = pl.ds(place * vocab + group * 128, 128)
                policy = softcap * jnp.tanh(policy_acc[rows, lanes] * (1.0 / softcap))
                reference = softcap * jnp.tanh(reference_acc[rows, lanes] * (1.0 / softcap))
                mixed = keep * policy + weight * reference
                diff_ref[rows, pl.ds(group * 128, 128)] = mixed - policy
                hit = lax.broadcasted_iota(jnp.int32, (8, 128), 1) + group * 128 == token
                terms = (
                    jnp.exp(policy),
                    jnp.exp(mixed),
                    jnp.exp(reference),
                    jnp.where(hit, policy, 0.0),
                    jnp.where(hit, reference, 0.0),
                )
                sums = [total + term for total, term in zip(sums, terms)]
        for k in range(5):
            partial[k, rows, :] = sums[k]
        return carry

    lax.fori_loop(0, seqs // 8, body, 0, unroll=8)
    sums = [jnp.sum(partial[k].T, axis=0, keepdims=True) for k in range(5)]
    whole = jnp.concatenate(sums[:2], axis=1)
    for shard in range(shards):
        start = shard * part // 128 * 128
        block_ref[shard] = jnp.concatenate(
            [whole] + [total[:, start : start + 128] for total in sums[2:]], axis=1
        )


def mixture(place, main, quarters, policy_own, policy_other, reference_own, reference_other, weight, token):
    shards, rows, width = main.shape
    part = rows // 3 * 2
    vocab = policy_own.shape[0]
    seqs = shards * part
    chunks = 7
    return pl.pallas_call(
        mixture_kernel,
        in_specs=[pl.BlockSpec(memory_space=pltpu.SMEM)] + [HBM] * 5 + [VMEM] + [HBM] * 3 + [VMEM] * 2,
        out_specs=[VMEM] * 3,
        out_shape=[
            jax.ShapeDtypeStruct((seqs, vocab), jnp.float32),
            jax.ShapeDtypeStruct((seqs, vocab), jnp.float32),
            jax.ShapeDtypeStruct((shards, 1, 2 * seqs + 3 * 128), jnp.float32),
        ],
        scratch_shapes=[
            pltpu.VMEM((shards, 2, part, width), jnp.bfloat16),
            pltpu.VMEM((3, vocab, width), jnp.bfloat16),
            pltpu.VMEM((seqs, 2 * vocab), jnp.float32),
            pltpu.VMEM((seqs, 2 * vocab), jnp.float32),
            pltpu.VMEM((5, seqs, 128), jnp.float32),
            pltpu.SemaphoreType.DMA((chunks, 5)),
            pltpu.SemaphoreType.DMA((4,)),
        ],
        compiler_params=pltpu.CompilerParams(vmem_limit_bytes=32 * MIB),
        name="mixture",
    )(
        place,
        in_hbm(main),
        *map(in_hbm, quarters),
        pltpu.with_memory_space_constraint(policy_own, pltpu.VMEM),
        in_hbm(policy_other),
        in_hbm(reference_own),
        in_hbm(reference_other),
        weight,
        token,
    )


def finish_kernel(columns, place_ref, own_ref, other_ref, blocks_ref, weight_ref, shift_ref, sampled_ref, staged, sem):
    shards, _, part, vocab = shift_ref.shape
    seqs = shards * part
    half = place_ref[0]
    shard = place_ref[1]

    totals = [None, None]
    for j in range(blocks_ref.shape[0]):
        k = half_bit(j // columns, j % columns)
        totals[k] = blocks_ref[j] if totals[k] is None else totals[k] + blocks_ref[j]
    logs = [jnp.log(total[:, : 2 * seqs + 128]) for total in totals]
    deltas = [log[:, :seqs] - log[:, seqs : 2 * seqs] for log in logs]
    own_first = half == 0
    turns = (
        jnp.where(own_first, deltas[0], deltas[1]),
        jnp.where(own_first, deltas[1], deltas[0]),
    )

    chunk = 128
    per = chunk // part
    stores = []
    for turn, diff_ref in enumerate((own_ref, other_ref)):
        target = half if turn == 0 else 1 - half
        for j in range(seqs // chunk):
            delta = jnp.broadcast_to(turns[turn][:, j * chunk : (j + 1) * chunk], (chunk, chunk)).T
            shards_here = pl.ds(j * per, per)
            for group in range(vocab // 128):
                lanes = pl.ds(group * 128, 128)
                shifted = diff_ref[pl.ds(j * chunk, chunk), lanes] + delta
                staged[turn, shards_here, :, lanes] = shifted.reshape(per, part, 128)
            store = pltpu.make_async_copy(
                staged.at[turn, shards_here],
                shift_ref.at[shards_here, target],
                sem.at[turn, j],
            )
            store.start()
            stores.append(store)

    mine = shard * part // 128
    picked = []
    for total, log in zip(totals, logs):
        policy = jnp.zeros((1, 128), jnp.float32)
        mixed = jnp.zeros((1, 128), jnp.float32)
        for j in range(seqs // 128):
            policy = jnp.where(mine == j, log[:, j * 128 : (j + 1) * 128], policy)
            mixed = jnp.where(mine == j, log[:, seqs + j * 128 : seqs + (j + 1) * 128], mixed)
        policy_pick = total[:, 2 * seqs + 128 : 2 * seqs + 256]
        reference_pick = total[:, 2 * seqs + 256 : 2 * seqs + 384]
        picked.append((policy_pick, reference_pick, policy, log[:, 2 * seqs :], mixed))
    lane = lax.broadcasted_iota(jnp.int32, (8, 128), 1)
    start = shard * part % 128
    values = []
    for low, high in zip(*picked):
        low = pltpu.roll(jnp.broadcast_to(low, (8, 128)), lax.rem(128 - start, 128), 1)
        high = pltpu.roll(jnp.broadcast_to(high, (8, 128)), lax.rem(128 + part - start, 128), 1)
        values.append(jnp.where(lane < part, low, high)[:1, : 2 * part])
    policy_pick, reference_pick, policy_log, reference_log, mixed_log = values
    weight = weight_ref[...]
    sampled_ref[0:1, :] = policy_pick - policy_log
    sampled_ref[1:2, :] = reference_pick - reference_log
    sampled_ref[2:3, :] = (1.0 - weight) * policy_pick + weight * reference_pick - mixed_log

    for store in stores:
        store.wait()


def finish(place, columns, diff_own, diff_other, blocks, weight, shards):
    seqs, vocab = diff_own.shape
    part = seqs // shards
    return pl.pallas_call(
        functools.partial(finish_kernel, columns),
        in_specs=[pl.BlockSpec(memory_space=pltpu.SMEM)] + [VMEM] * 4,
        out_specs=[HBM, VMEM],
        out_shape=[
            jax.ShapeDtypeStruct((shards, 2, part, vocab), jnp.float32),
            jax.ShapeDtypeStruct((3, 2 * part), jnp.float32),
        ],
        scratch_shapes=[
            pltpu.VMEM((2, shards, part, vocab), jnp.float32),
            pltpu.SemaphoreType.DMA((2, seqs // 128)),
        ],
        compiler_params=pltpu.CompilerParams(vmem_limit_bytes=16 * MIB),
        name="finish",
    )(place, diff_own, diff_other, blocks, weight)


def half_bit(row, column):
    return ((row + 1) // 2 + (column + 1) // 2) % 2


def beside(i, size):
    return (i + 1) % size if i % 2 else (i - 1) % size


def pairs_of(sizes, target):
    z, y, x = sizes
    pairs = []
    for source in range(z * 2 * y * x):
        i, rest = divmod(source, 2 * y * x)
        c, rest = divmod(rest, y * x)
        j, k = target(c, *divmod(rest, x))
        pairs.append((source, ((i * 2 + c) * y + j) * x + k))
    return pairs


def local(
    policy_hidden,
    reference_hidden,
    policy_gain,
    reference_gain,
    policy_embedding,
    reference_embedding,
    mixture_weight,
    sampled_tokens,
):
    seq_local = policy_hidden.shape[0]
    part = seq_local // 2
    vocab = policy_embedding.shape[0]
    shards = lax.axis_size(DP)
    copies = lax.axis_size(MP)
    shard = lax.axis_index(DP)
    copy = lax.axis_index(MP)
    core = lax.axis_index("dp_1")
    row = lax.axis_index("mp_0")
    column = lax.axis_index("mp_1")
    half = half_bit(row, column)
    quarter = 3 - 2 * (row % 2) - column % 2
    other_copy = jnp.where(
        core == 0,
        row * lax.axis_size("mp_1") + (column ^ 1),
        (row ^ 1) * lax.axis_size("mp_1") + column,
    )
    first_own = (shard * copies + copy) * vocab
    first_other = (shard * copies + other_copy) * vocab
    place = jnp.stack([half, shard, quarter]).astype(jnp.int32)
    sizes = lax.axis_size("dp_0"), lax.axis_size("mp_0"), lax.axis_size("mp_1")
    pairs = pairs_of(sizes, lambda c, j, k: (j, k ^ 1) if c == 0 else (j ^ 1, k))
    beyond = pairs_of(
        sizes, lambda c, j, k: (j, beside(k, sizes[2])) if c == 0 else (beside(j, sizes[1]), k)
    )
    aslant = pairs_of(sizes, lambda c, j, k: (beside(j, sizes[1]), beside(k, sizes[2])))

    main, part_quarter = normalize(place, policy_hidden, reference_hidden, policy_gain, reference_gain)
    main, part_quarter, policy_send, reference_send = lax.optimization_barrier(
        (main, part_quarter, policy_embedding, reference_embedding)
    )
    main = lax.all_gather(main, DP, axis=0)
    policy_other = lax.ppermute(policy_send, DP_MP, pairs)
    reference_other = lax.ppermute(reference_send, DP_MP, pairs)
    held = lax.all_gather(part_quarter, DP, axis=0)
    fetched = lax.ppermute(held, DP_MP, beyond)
    opposite = lax.ppermute(held, DP_MP, aslant)
    swapped = lax.ppermute(fetched, "dp_1", [(0, 1), (1, 0)])
    quarters = [held, fetched, swapped, opposite]

    seqs = shards * part
    weights = mixture_weight.reshape(shards, 2, part)
    tokens = sampled_tokens.reshape(shards, 2, part)
    weight = lax.dynamic_index_in_dim(weights, half, 1, False).reshape(seqs, 1)
    token = lax.dynamic_index_in_dim(tokens, half, 1, False).reshape(seqs, 1)
    token = jnp.stack([token - first_own, token - first_other])
    weight = jnp.broadcast_to(weight, (seqs, 128))
    token = jnp.broadcast_to(token, (2, seqs, 128))
    weight_mine = lax.dynamic_slice_in_dim(mixture_weight, shard * seq_local, seq_local)[None]
    policy_other, reference_other, weight, token = lax.optimization_barrier(
        (policy_other, reference_other, weight, token)
    )
    diff_own, diff_send, block = mixture(
        place, main, quarters, policy_embedding, policy_other, reference_embedding, reference_other, weight, token
    )

    block = lax.all_to_all(block, DP, 0, 0, tiled=True)
    block, diff_send = lax.optimization_barrier((block, diff_send))
    diff_other = lax.ppermute(diff_send, DP_MP, pairs)
    block = jnp.sum(block, axis=0, keepdims=True)
    block = jnp.broadcast_to(block, (copies,) + block.shape[1:])
    blocks = lax.all_to_all(block, MP, 0, 0, tiled=True)
    mixture_shift, sampled_logprobs = finish(
        place, lax.axis_size("mp_1"), diff_own, diff_other, blocks, weight_mine, shards
    )
    return (mixture_shift.reshape(shards * seq_local, vocab), sampled_logprobs)


def solution(mesh):
    split = Mesh(mesh.devices.reshape(8, 2, 8, 4), ("dp_0", "dp_1", "mp_0", "mp_1"))
    in_specs = (P(DP, None), P(DP, None), P(), P(), P(DP_MP, None), P(DP_MP, None), P(), P())
    out_specs = (P(None, DP_MP), P(None, DP))
    return jax.shard_map(local, mesh=split, in_specs=in_specs, out_specs=out_specs, check_vma=False)
```

```python
import functools

import jax
import jax.numpy as jnp
from jax import lax
from jax.experimental import pallas as pl
from jax.experimental.pallas import tpu as pltpu
from jax.sharding import Mesh
from jax.sharding import PartitionSpec as P

DP = ("dp_0", "dp_1")
MP = ("mp_0", "mp_1")
DP_MP = ("dp_0", "dp_1", "mp_0", "mp_1")

softcap = 30.0
epsilon = 1e-06

MIB = 1024 * 1024
HBM = pl.BlockSpec(memory_space=pltpu.HBM)
VMEM = pl.BlockSpec(memory_space=pltpu.VMEM)


def in_hbm(x):
    return pltpu.with_memory_space_constraint(x, pltpu.HBM)


def normalize_kernel(
    place_ref, policy_ref, reference_ref, policy_gain_ref, reference_gain_ref, main_ref, quarter_ref, rows, in_sem
):
    part, width = rows.shape[1:]
    depth = width // 4
    first = pl.multiple_of(place_ref[0] * part, part)
    models = ((policy_ref, policy_gain_ref), (reference_ref, reference_gain_ref))
    loads = [
        pltpu.make_async_copy(hidden_ref.at[pl.ds(first, part), :], rows.at[model], in_sem.at[model])
        for model, (hidden_ref, _) in enumerate(models)
    ]
    for load in loads:
        load.start()
    for model, (_, gain_ref) in enumerate(models):
        loads[model].wait()
        values = rows[model].astype(jnp.float32)
        meansq = jnp.mean(values * values, axis=-1, keepdims=True)
        gain = gain_ref[...].reshape(1, width)
        normed = (values * lax.rsqrt(meansq + epsilon) * gain).astype(jnp.bfloat16)
        if model == 0:
            main_ref[: part // 2] = normed[: part // 2]
            for i in range(4):

                @pl.when(place_ref[2] == i)
                def _(i=i, normed=normed):
                    quarter_ref[...] = normed[part // 2 :, i * depth : (i + 1) * depth]
        else:
            main_ref[part // 2 :] = normed


def normalize(place, policy_hidden, reference_hidden, policy_gain, reference_gain):
    rows, width = policy_hidden.shape
    part = rows // 2
    return pl.pallas_call(
        normalize_kernel,
        in_specs=[pl.BlockSpec(memory_space=pltpu.SMEM)] + [HBM] * 2 + [VMEM] * 2,
        out_specs=[VMEM] * 2,
        out_shape=[
            jax.ShapeDtypeStruct((part + part // 2, width), jnp.bfloat16),
            jax.ShapeDtypeStruct((part // 2, width // 4), jnp.bfloat16),
        ],
        scratch_shapes=[pltpu.VMEM((2, part, width), jnp.bfloat16), pltpu.SemaphoreType.DMA((2,))],
        compiler_params=pltpu.CompilerParams(vmem_limit_bytes=16 * MIB),
        name="normalize",
    )(place, in_hbm(policy_hidden), in_hbm(reference_hidden), in_hbm(policy_gain), in_hbm(reference_gain))


def mixture_kernel(
    place_ref,
    main_ref,
    quarter_0_ref,
    quarter_1_ref,
    quarter_2_ref,
    quarter_3_ref,
    policy_own_ref,
    policy_other_ref,
    reference_own_ref,
    reference_other_ref,
    weight_ref,
    token_ref,
    diff_own_ref,
    diff_other_ref,
    block_ref,
    hidden,
    loaded,
    policy_acc,
    reference_acc,
    partial,
    sem,
    quarter_sem,
):
    chunks = sem.shape[0]
    shards, _, part, width = hidden.shape
    depth = width // chunks
    vocab = policy_own_ref.shape[0]
    seqs = shards * part

    def loads(model, k):
        columns = pl.ds(k * depth, depth)
        low, high = pl.ds(0, part // 2), pl.ds(part // 2, part)
        if model == 0:
            pairs = [
                (main_ref.at[:, low, columns], hidden.at[:, 0, low, columns]),
                (policy_other_ref.at[:, columns], loaded.at[0, :, columns]),
            ]
        else:
            pairs = [
                (main_ref.at[:, high, columns], hidden.at[:, 1, :, columns]),
                (reference_own_ref.at[:, columns], loaded.at[1, :, columns]),
                (reference_other_ref.at[:, columns], loaded.at[2, :, columns]),
            ]
        return [pltpu.make_async_copy(*pair, sem.at[model, k, i]) for i, pair in enumerate(pairs)]

    quarters = []
    core = place_ref[1] % 2
    flips = (0, 1 + core, 2 - core, 3)
    for i, ref in enumerate((quarter_0_ref, quarter_1_ref, quarter_2_ref, quarter_3_ref)):
        start = pl.multiple_of((place_ref[2] ^ flips[i]) * (width // 4), 128)
        target = hidden.at[:, 0, pl.ds(part // 2, part // 2), pl.ds(start, width // 4)]
        quarters.append(pltpu.make_async_copy(ref, target, quarter_sem.at[i]))
    for k in range(chunks):
        for load in loads(1, k):
            load.start()
    for quarter in quarters:
        quarter.start()
    for k in range(chunks):
        for load in loads(0, k):
            load.start()
    for model, acc in ((1, reference_acc), (0, policy_acc)):
        if model == 0:
            for quarter in quarters:
                quarter.wait()
        for k in range(chunks):
            for load in loads(model, k):
                load.wait()
            columns = pl.ds(k * depth, depth)
            left = hidden[:, model, :, columns].reshape(seqs, depth)
            for place in range(2):
                index = 2 * model + place
                rows = policy_own_ref[:, columns] if index == 0 else loaded[index - 1, :, columns]
                product = lax.dot_general(
                    left, rows, (((1,), (1,)), ((), ())), preferred_element_type=jnp.float32
                )
                target = pl.ds(place * vocab, vocab)
                acc[:, target] = product if k == 0 else acc[:, target] + product

    def body(i, carry):
        rows = pl.ds(pl.multiple_of(i * 8, 8), 8)
        weight = weight_ref[rows, :]
        keep = 1.0 - weight
        sums = [jnp.zeros((8, 128), jnp.float32) for _ in range(5)]
        for place, diff_ref in enumerate((diff_own_ref, diff_other_ref)):
            token = token_ref[place, rows, :]
            for group in range(vocab // 128):
                lanes = pl.ds(place * vocab + group * 128, 128)
                policy = softcap * jnp.tanh(policy_acc[rows, lanes] * (1.0 / softcap))
                reference = softcap * jnp.tanh(reference_acc[rows, lanes] * (1.0 / softcap))
                mixed = keep * policy + weight * reference
                diff_ref[rows, pl.ds(group * 128, 128)] = mixed - policy
                hit = lax.broadcasted_iota(jnp.int32, (8, 128), 1) + group * 128 == token
                terms = (
                    jnp.exp(policy),
                    jnp.exp(mixed),
                    jnp.exp(reference),
                    jnp.where(hit, policy, 0.0),
                    jnp.where(hit, reference, 0.0),
                )
                sums = [total + term for total, term in zip(sums, terms)]
        for k in range(5):
            partial[k, rows, :] = sums[k]
        return carry

    lax.fori_loop(0, seqs // 8, body, 0, unroll=8)
    sums = [jnp.sum(partial[k].T, axis=0, keepdims=True) for k in range(5)]
    whole = jnp.concatenate(sums[:2], axis=1)
    for shard in range(shards):
        start = shard * part // 128 * 128
        block_ref[shard] = jnp.concatenate(
            [whole] + [total[:, start : start + 128] for total in sums[2:]], axis=1
        )


def mixture(place, main, quarters, policy_own, policy_other, reference_own, reference_other, weight, token):
    shards, rows, width = main.shape
    part = rows // 3 * 2
    vocab = policy_own.shape[0]
    seqs = shards * part
    chunks = 7
    return pl.pallas_call(
        mixture_kernel,
        in_specs=[pl.BlockSpec(memory_space=pltpu.SMEM)] + [HBM] * 5 + [VMEM] + [HBM] * 3 + [VMEM] * 2,
        out_specs=[VMEM] * 3,
        out_shape=[
            jax.ShapeDtypeStruct((seqs, vocab), jnp.float32),
            jax.ShapeDtypeStruct((seqs, vocab), jnp.float32),
            jax.ShapeDtypeStruct((shards, 1, 2 * seqs + 3 * 128), jnp.float32),
        ],
        scratch_shapes=[
            pltpu.VMEM((shards, 2, part, width), jnp.bfloat16),
            pltpu.VMEM((3, vocab, width), jnp.bfloat16),
            pltpu.VMEM((seqs, 2 * vocab), jnp.float32),
            pltpu.VMEM((seqs, 2 * vocab), jnp.float32),
            pltpu.VMEM((5, seqs, 128), jnp.float32),
            pltpu.SemaphoreType.DMA((2, chunks, 3)),
            pltpu.SemaphoreType.DMA((4,)),
        ],
        compiler_params=pltpu.CompilerParams(vmem_limit_bytes=32 * MIB),
        name="mixture",
    )(
        place,
        in_hbm(main),
        *map(in_hbm, quarters),
        pltpu.with_memory_space_constraint(policy_own, pltpu.VMEM),
        in_hbm(policy_other),
        in_hbm(reference_own),
        in_hbm(reference_other),
        weight,
        token,
    )


def finish_kernel(columns, place_ref, own_ref, other_ref, blocks_ref, weight_ref, shift_ref, sampled_ref, staged, sem):
    shards, _, part, vocab = shift_ref.shape
    seqs = shards * part
    half = place_ref[0]
    shard = place_ref[1]

    totals = [None, None]
    for j in range(blocks_ref.shape[0]):
        k = half_bit(j // columns, j % columns)
        totals[k] = blocks_ref[j] if totals[k] is None else totals[k] + blocks_ref[j]
    logs = [jnp.log(total[:, : 2 * seqs + 128]) for total in totals]
    deltas = [log[:, :seqs] - log[:, seqs : 2 * seqs] for log in logs]
    own_first = half == 0
    turns = (
        jnp.where(own_first, deltas[0], deltas[1]),
        jnp.where(own_first, deltas[1], deltas[0]),
    )

    chunk = 128
    per = chunk // part
    stores = []
    for turn, diff_ref in enumerate((own_ref, other_ref)):
        target = half if turn == 0 else 1 - half
        for j in range(seqs // chunk):
            delta = jnp.broadcast_to(turns[turn][:, j * chunk : (j + 1) * chunk], (chunk, chunk)).T
            shards_here = pl.ds(j * per, per)
            for group in range(vocab // 128):
                lanes = pl.ds(group * 128, 128)
                shifted = diff_ref[pl.ds(j * chunk, chunk), lanes] + delta
                staged[turn, shards_here, :, lanes] = shifted.reshape(per, part, 128)
            store = pltpu.make_async_copy(
                staged.at[turn, shards_here],
                shift_ref.at[shards_here, target],
                sem.at[turn, j],
            )
            store.start()
            stores.append(store)

    mine = shard * part // 128
    picked = []
    for total, log in zip(totals, logs):
        policy = jnp.zeros((1, 128), jnp.float32)
        mixed = jnp.zeros((1, 128), jnp.float32)
        for j in range(seqs // 128):
            policy = jnp.where(mine == j, log[:, j * 128 : (j + 1) * 128], policy)
            mixed = jnp.where(mine == j, log[:, seqs + j * 128 : seqs + (j + 1) * 128], mixed)
        policy_pick = total[:, 2 * seqs + 128 : 2 * seqs + 256]
        reference_pick = total[:, 2 * seqs + 256 : 2 * seqs + 384]
        picked.append((policy_pick, reference_pick, policy, log[:, 2 * seqs :], mixed))
    lane = lax.broadcasted_iota(jnp.int32, (8, 128), 1)
    start = shard * part % 128
    values = []
    for low, high in zip(*picked):
        low = pltpu.roll(jnp.broadcast_to(low, (8, 128)), lax.rem(128 - start, 128), 1)
        high = pltpu.roll(jnp.broadcast_to(high, (8, 128)), lax.rem(128 + part - start, 128), 1)
        values.append(jnp.where(lane < part, low, high)[:1, : 2 * part])
    policy_pick, reference_pick, policy_log, reference_log, mixed_log = values
    weight = weight_ref[...]
    sampled_ref[0:1, :] = policy_pick - policy_log
    sampled_ref[1:2, :] = reference_pick - reference_log
    sampled_ref[2:3, :] = (1.0 - weight) * policy_pick + weight * reference_pick - mixed_log

    for store in stores:
        store.wait()


def finish(place, columns, diff_own, diff_other, blocks, weight, shards):
    seqs, vocab = diff_own.shape
    part = seqs // shards
    return pl.pallas_call(
        functools.partial(finish_kernel, columns),
        in_specs=[pl.BlockSpec(memory_space=pltpu.SMEM)] + [VMEM] * 4,
        out_specs=[HBM, VMEM],
        out_shape=[
            jax.ShapeDtypeStruct((shards, 2, part, vocab), jnp.float32),
            jax.ShapeDtypeStruct((3, 2 * part), jnp.float32),
        ],
        scratch_shapes=[
            pltpu.VMEM((2, shards, part, vocab), jnp.float32),
            pltpu.SemaphoreType.DMA((2, seqs // 128)),
        ],
        compiler_params=pltpu.CompilerParams(vmem_limit_bytes=16 * MIB),
        name="finish",
    )(place, diff_own, diff_other, blocks, weight)


def half_bit(row, column):
    return ((row + 1) // 2 + (column + 1) // 2) % 2


def beside(i, size):
    return (i + 1) % size if i % 2 else (i - 1) % size


def pairs_of(sizes, target):
    z, y, x = sizes
    pairs = []
    for source in range(z * 2 * y * x):
        i, rest = divmod(source, 2 * y * x)
        c, rest = divmod(rest, y * x)
        j, k = target(c, *divmod(rest, x))
        pairs.append((source, ((i * 2 + c) * y + j) * x + k))
    return pairs


def local(
    policy_hidden,
    reference_hidden,
    policy_gain,
    reference_gain,
    policy_embedding,
    reference_embedding,
    mixture_weight,
    sampled_tokens,
):
    seq_local = policy_hidden.shape[0]
    part = seq_local // 2
    vocab = policy_embedding.shape[0]
    shards = lax.axis_size(DP)
    copies = lax.axis_size(MP)
    shard = lax.axis_index(DP)
    copy = lax.axis_index(MP)
    core = lax.axis_index("dp_1")
    row = lax.axis_index("mp_0")
    column = lax.axis_index("mp_1")
    half = half_bit(row, column)
    quarter = 3 - 2 * (row % 2) - column % 2
    other_copy = jnp.where(
        core == 0,
        row * lax.axis_size("mp_1") + (column ^ 1),
        (row ^ 1) * lax.axis_size("mp_1") + column,
    )
    first_own = (shard * copies + copy) * vocab
    first_other = (shard * copies + other_copy) * vocab
    place = jnp.stack([half, shard, quarter]).astype(jnp.int32)
    sizes = lax.axis_size("dp_0"), lax.axis_size("mp_0"), lax.axis_size("mp_1")
    pairs = pairs_of(sizes, lambda c, j, k: (j, k ^ 1) if c == 0 else (j ^ 1, k))
    beyond = pairs_of(
        sizes, lambda c, j, k: (j, beside(k, sizes[2])) if c == 0 else (beside(j, sizes[1]), k)
    )
    aslant = pairs_of(sizes, lambda c, j, k: (beside(j, sizes[1]), beside(k, sizes[2])))

    main, part_quarter = normalize(place, policy_hidden, reference_hidden, policy_gain, reference_gain)
    main, part_quarter, policy_send, reference_send = lax.optimization_barrier(
        (main, part_quarter, policy_embedding, reference_embedding)
    )
    main = lax.all_gather(main, DP, axis=0)
    policy_other = lax.ppermute(policy_send, DP_MP, pairs)
    reference_other = lax.ppermute(reference_send, DP_MP, pairs)
    held = lax.all_gather(part_quarter, DP, axis=0)
    fetched = lax.ppermute(held, DP_MP, beyond)
    opposite = lax.ppermute(held, DP_MP, aslant)
    swapped = lax.ppermute(fetched, "dp_1", [(0, 1), (1, 0)])
    quarters = [held, fetched, swapped, opposite]

    seqs = shards * part
    weights = mixture_weight.reshape(shards, 2, part)
    tokens = sampled_tokens.reshape(shards, 2, part)
    weight = lax.dynamic_index_in_dim(weights, half, 1, False).reshape(seqs, 1)
    token = lax.dynamic_index_in_dim(tokens, half, 1, False).reshape(seqs, 1)
    token = jnp.stack([token - first_own, token - first_other])
    weight = jnp.broadcast_to(weight, (seqs, 128))
    token = jnp.broadcast_to(token, (2, seqs, 128))
    weight_mine = lax.dynamic_slice_in_dim(mixture_weight, shard * seq_local, seq_local)[None]
    policy_other, reference_other, weight, token = lax.optimization_barrier(
        (policy_other, reference_other, weight, token)
    )
    diff_own, diff_send, block = mixture(
        place, main, quarters, policy_embedding, policy_other, reference_embedding, reference_other, weight, token
    )

    block = lax.all_to_all(block, DP, 0, 0, tiled=True)
    block, diff_send = lax.optimization_barrier((block, diff_send))
    diff_other = lax.ppermute(diff_send, DP_MP, pairs)
    block = jnp.sum(block, axis=0, keepdims=True)
    block = jnp.broadcast_to(block, (copies,) + block.shape[1:])
    blocks = lax.all_to_all(block, MP, 0, 0, tiled=True)
    mixture_shift, sampled_logprobs = finish(
        place, lax.axis_size("mp_1"), diff_own, diff_other, blocks, weight_mine, shards
    )
    return (mixture_shift.reshape(shards * seq_local, vocab), sampled_logprobs)


def solution(mesh):
    split = Mesh(mesh.devices.reshape(8, 2, 8, 4), ("dp_0", "dp_1", "mp_0", "mp_1"))
    in_specs = (P(DP, None), P(DP, None), P(), P(), P(DP_MP, None), P(DP_MP, None), P(), P())
    out_specs = (P(None, DP_MP), P(None, DP))
    return jax.shard_map(local, mesh=split, in_specs=in_specs, out_specs=out_specs, check_vma=False)
```

```python
import functools

import jax
import jax.numpy as jnp
from jax import lax
from jax.experimental import pallas as pl
from jax.experimental.pallas import tpu as pltpu
from jax.sharding import Mesh
from jax.sharding import PartitionSpec as P

DP = ("dp_0", "dp_1")
MP = ("mp_0", "mp_1")
DP_MP = ("dp_0", "dp_1", "mp_0", "mp_1")

softcap = 30.0
epsilon = 1e-06

MIB = 1024 * 1024
HBM = pl.BlockSpec(memory_space=pltpu.HBM)
VMEM = pl.BlockSpec(memory_space=pltpu.VMEM)


def in_hbm(x):
    return pltpu.with_memory_space_constraint(x, pltpu.HBM)


def normalize_kernel(
    place_ref, policy_ref, reference_ref, policy_gain_ref, reference_gain_ref, main_ref, quarter_ref, rows, in_sem
):
    part, width = rows.shape[1:]
    depth = width // 4
    first = pl.multiple_of(place_ref[0] * part, part)
    models = ((policy_ref, policy_gain_ref), (reference_ref, reference_gain_ref))
    loads = [
        pltpu.make_async_copy(hidden_ref.at[pl.ds(first, part), :], rows.at[model], in_sem.at[model])
        for model, (hidden_ref, _) in enumerate(models)
    ]
    for load in loads:
        load.start()
    for model, (_, gain_ref) in enumerate(models):
        loads[model].wait()
        values = rows[model].astype(jnp.float32)
        meansq = jnp.mean(values * values, axis=-1, keepdims=True)
        gain = gain_ref[...].reshape(1, width)
        normed = (values * lax.rsqrt(meansq + epsilon) * gain).astype(jnp.bfloat16)
        if model == 0:
            main_ref[: part // 2] = normed[: part // 2]
            for i in range(4):

                @pl.when(place_ref[2] == i)
                def _(i=i, normed=normed):
                    quarter_ref[...] = normed[part // 2 :, i * depth : (i + 1) * depth]
        else:
            main_ref[part // 2 :] = normed


def normalize(place, policy_hidden, reference_hidden, policy_gain, reference_gain):
    rows, width = policy_hidden.shape
    part = rows // 2
    return pl.pallas_call(
        normalize_kernel,
        in_specs=[pl.BlockSpec(memory_space=pltpu.SMEM)] + [HBM] * 2 + [VMEM] * 2,
        out_specs=[VMEM] * 2,
        out_shape=[
            jax.ShapeDtypeStruct((part + part // 2, width), jnp.bfloat16),
            jax.ShapeDtypeStruct((part // 2, width // 4), jnp.bfloat16),
        ],
        scratch_shapes=[pltpu.VMEM((2, part, width), jnp.bfloat16), pltpu.SemaphoreType.DMA((2,))],
        compiler_params=pltpu.CompilerParams(vmem_limit_bytes=16 * MIB),
        name="normalize",
    )(place, in_hbm(policy_hidden), in_hbm(reference_hidden), in_hbm(policy_gain), in_hbm(reference_gain))


def mixture_kernel(
    place_ref,
    main_ref,
    quarter_0_ref,
    quarter_1_ref,
    quarter_2_ref,
    quarter_3_ref,
    policy_own_ref,
    policy_other_ref,
    reference_own_ref,
    reference_other_ref,
    weight_ref,
    token_ref,
    diff_own_ref,
    diff_other_ref,
    block_ref,
    hidden,
    loaded,
    policy_acc,
    reference_acc,
    partial,
    sem,
    quarter_sem,
):
    chunks = sem.shape[0]
    shards, _, part, width = hidden.shape
    depth = width // chunks
    vocab = policy_own_ref.shape[0]
    seqs = shards * part

    def loads(k):
        columns = pl.ds(k * depth, depth)
        low = pl.ds(0, part // 2)
        rest = (policy_other_ref, reference_own_ref, reference_other_ref)
        pairs = [
            (main_ref.at[:, low, columns], hidden.at[:, 0, low, columns]),
            (main_ref.at[:, pl.ds(part // 2, part), columns], hidden.at[:, 1, :, columns]),
        ]
        pairs += [(ref.at[:, columns], loaded.at[i, :, columns]) for i, ref in enumerate(rest)]
        return [pltpu.make_async_copy(*pair, sem.at[k, i]) for i, pair in enumerate(pairs)]

    quarters = []
    core = place_ref[1] % 2
    flips = (0, 1 + core, 2 - core, 3)
    for i, ref in enumerate((quarter_0_ref, quarter_1_ref, quarter_2_ref, quarter_3_ref)):
        start = pl.multiple_of((place_ref[2] ^ flips[i]) * (width // 4), 128)
        target = hidden.at[:, 0, pl.ds(part // 2, part // 2), pl.ds(start, width // 4)]
        quarters.append(pltpu.make_async_copy(ref, target, quarter_sem.at[i]))
    for quarter in quarters:
        quarter.start()
    for k in range(chunks):
        for load in loads(k):
            load.start()
    for quarter in quarters:
        quarter.wait()
    for k in range(chunks):
        for load in loads(k):
            load.wait()
        columns = pl.ds(k * depth, depth)
        for model, acc in enumerate((policy_acc, reference_acc)):
            left = hidden[:, model, :, columns].reshape(seqs, depth)
            for place in range(2):
                index = 2 * model + place
                rows = policy_own_ref[:, columns] if index == 0 else loaded[index - 1, :, columns]
                product = lax.dot_general(
                    left, rows, (((1,), (1,)), ((), ())), preferred_element_type=jnp.float32
                )
                target = pl.ds(place * vocab, vocab)
                acc[:, target] = product if k == 0 else acc[:, target] + product

    def body(i, carry):
        rows = pl.ds(pl.multiple_of(i * 8, 8), 8)
        weight = weight_ref[rows, :]
        keep = 1.0 - weight
        sums = [jnp.zeros((8, 128), jnp.float32) for _ in range(5)]
        for place, diff_ref in enumerate((diff_own_ref, diff_other_ref)):
            token = token_ref[place, rows, :]
            for group in range(vocab // 128):
                lanes = pl.ds(place * vocab + group * 128, 128)
                policy = softcap * jnp.tanh(policy_acc[rows, lanes] * (1.0 / softcap))
                reference = softcap * jnp.tanh(reference_acc[rows, lanes] * (1.0 / softcap))
                mixed = keep * policy + weight * reference
                diff_ref[rows, pl.ds(group * 128, 128)] = mixed - policy
                hit = lax.broadcasted_iota(jnp.int32, (8, 128), 1) + group * 128 == token
                terms = (
                    jnp.exp(policy),
                    jnp.exp(mixed),
                    jnp.exp(reference),
                    jnp.where(hit, policy, 0.0),
                    jnp.where(hit, reference, 0.0),
                )
                sums = [total + term for total, term in zip(sums, terms)]
        for k in range(5):
            partial[k, rows, :] = sums[k]
        return carry

    lax.fori_loop(0, seqs // 8, body, 0, unroll=8)
    sums = [jnp.sum(partial[k].T, axis=0, keepdims=True) for k in range(5)]
    whole = jnp.concatenate(sums[:2], axis=1)
    for shard in range(shards):
        start = shard * part // 128 * 128
        block_ref[shard] = jnp.concatenate(
            [whole] + [total[:, start : start + 128] for total in sums[2:]], axis=1
        )


def mixture(place, main, quarters, policy_own, policy_other, reference_own, reference_other, weight, token):
    shards, rows, width = main.shape
    part = rows // 3 * 2
    vocab = policy_own.shape[0]
    seqs = shards * part
    chunks = 7
    return pl.pallas_call(
        mixture_kernel,
        in_specs=[pl.BlockSpec(memory_space=pltpu.SMEM)] + [HBM] * 5 + [VMEM] + [HBM] * 3 + [VMEM] * 2,
        out_specs=[VMEM] * 3,
        out_shape=[
            jax.ShapeDtypeStruct((seqs, vocab), jnp.float32),
            jax.ShapeDtypeStruct((seqs, vocab), jnp.float32),
            jax.ShapeDtypeStruct((shards, 1, 2 * seqs + 3 * 128), jnp.float32),
        ],
        scratch_shapes=[
            pltpu.VMEM((shards, 2, part, width), jnp.bfloat16),
            pltpu.VMEM((3, vocab, width), jnp.bfloat16),
            pltpu.VMEM((seqs, 2 * vocab), jnp.float32),
            pltpu.VMEM((seqs, 2 * vocab), jnp.float32),
            pltpu.VMEM((5, seqs, 128), jnp.float32),
            pltpu.SemaphoreType.DMA((chunks, 5)),
            pltpu.SemaphoreType.DMA((4,)),
        ],
        compiler_params=pltpu.CompilerParams(vmem_limit_bytes=32 * MIB),
        name="mixture",
    )(
        place,
        in_hbm(main),
        *map(in_hbm, quarters),
        pltpu.with_memory_space_constraint(policy_own, pltpu.VMEM),
        in_hbm(policy_other),
        in_hbm(reference_own),
        in_hbm(reference_other),
        weight,
        token,
    )


def finish_kernel(columns, place_ref, own_ref, other_ref, blocks_ref, weight_ref, shift_ref, sampled_ref, staged, sem):
    shards, _, part, vocab = shift_ref.shape
    seqs = shards * part
    half = place_ref[0]
    shard = place_ref[1]

    totals = [None, None]
    for j in range(blocks_ref.shape[0]):
        k = half_bit(j // columns, j % columns)
        totals[k] = blocks_ref[j] if totals[k] is None else totals[k] + blocks_ref[j]
    logs = [jnp.log(total[:, : 2 * seqs + 128]) for total in totals]
    deltas = [log[:, :seqs] - log[:, seqs : 2 * seqs] for log in logs]
    own_first = half == 0
    turns = (
        jnp.where(own_first, deltas[0], deltas[1]),
        jnp.where(own_first, deltas[1], deltas[0]),
    )

    chunk = 128
    per = chunk // part
    stores = []
    for turn, diff_ref in enumerate((own_ref, other_ref)):
        target = half if turn == 0 else 1 - half
        for j in range(seqs // chunk):
            delta = jnp.broadcast_to(turns[turn][:, j * chunk : (j + 1) * chunk], (chunk, chunk)).T
            shards_here = pl.ds(j * per, per)
            for group in range(vocab // 128):
                lanes = pl.ds(group * 128, 128)
                shifted = diff_ref[pl.ds(j * chunk, chunk), lanes] + delta
                staged[turn, shards_here, :, lanes] = shifted.reshape(per, part, 128)
            store = pltpu.make_async_copy(
                staged.at[turn, shards_here],
                shift_ref.at[shards_here, target],
                sem.at[turn, j],
            )
            store.start()
            stores.append(store)

    mine = shard * part // 128
    picked = []
    for total, log in zip(totals, logs):
        policy = jnp.zeros((1, 128), jnp.float32)
        mixed = jnp.zeros((1, 128), jnp.float32)
        for j in range(seqs // 128):
            policy = jnp.where(mine == j, log[:, j * 128 : (j + 1) * 128], policy)
            mixed = jnp.where(mine == j, log[:, seqs + j * 128 : seqs + (j + 1) * 128], mixed)
        policy_pick = total[:, 2 * seqs + 128 : 2 * seqs + 256]
        reference_pick = total[:, 2 * seqs + 256 : 2 * seqs + 384]
        picked.append((policy_pick, reference_pick, policy, log[:, 2 * seqs :], mixed))
    lane = lax.broadcasted_iota(jnp.int32, (8, 128), 1)
    start = shard * part % 128
    values = []
    for low, high in zip(*picked):
        low = pltpu.roll(jnp.broadcast_to(low, (8, 128)), lax.rem(128 - start, 128), 1)
        high = pltpu.roll(jnp.broadcast_to(high, (8, 128)), lax.rem(128 + part - start, 128), 1)
        values.append(jnp.where(lane < part, low, high)[:1, : 2 * part])
    policy_pick, reference_pick, policy_log, reference_log, mixed_log = values
    weight = weight_ref[...]
    sampled_ref[0:1, :] = policy_pick - policy_log
    sampled_ref[1:2, :] = reference_pick - reference_log
    sampled_ref[2:3, :] = (1.0 - weight) * policy_pick + weight * reference_pick - mixed_log

    for store in stores:
        store.wait()


def finish(place, columns, diff_own, diff_other, blocks, weight, shards):
    seqs, vocab = diff_own.shape
    part = seqs // shards
    return pl.pallas_call(
        functools.partial(finish_kernel, columns),
        in_specs=[pl.BlockSpec(memory_space=pltpu.SMEM)] + [VMEM] * 4,
        out_specs=[HBM, VMEM],
        out_shape=[
            jax.ShapeDtypeStruct((shards, 2, part, vocab), jnp.float32),
            jax.ShapeDtypeStruct((3, 2 * part), jnp.float32),
        ],
        scratch_shapes=[
            pltpu.VMEM((2, shards, part, vocab), jnp.float32),
            pltpu.SemaphoreType.DMA((2, seqs // 128)),
        ],
        compiler_params=pltpu.CompilerParams(vmem_limit_bytes=16 * MIB),
        name="finish",
    )(place, diff_own, diff_other, blocks, weight)


def half_bit(row, column):
    return ((row + 1) // 2 + (column + 1) // 2) % 2


def beside(i, size):
    return (i + 1) % size if i % 2 else (i - 1) % size


def pairs_of(sizes, target):
    z, y, x = sizes
    pairs = []
    for source in range(z * 2 * y * x):
        i, rest = divmod(source, 2 * y * x)
        c, rest = divmod(rest, y * x)
        j, k = target(c, *divmod(rest, x))
        pairs.append((source, ((i * 2 + c) * y + j) * x + k))
    return pairs


def local(
    policy_hidden,
    reference_hidden,
    policy_gain,
    reference_gain,
    policy_embedding,
    reference_embedding,
    mixture_weight,
    sampled_tokens,
):
    seq_local = policy_hidden.shape[0]
    part = seq_local // 2
    vocab = policy_embedding.shape[0]
    shards = lax.axis_size(DP)
    copies = lax.axis_size(MP)
    shard = lax.axis_index(DP)
    copy = lax.axis_index(MP)
    core = lax.axis_index("dp_1")
    row = lax.axis_index("mp_0")
    column = lax.axis_index("mp_1")
    half = half_bit(row, column)
    quarter = 3 - 2 * (row % 2) - column % 2
    other_copy = jnp.where(
        core == 0,
        row * lax.axis_size("mp_1") + (column ^ 1),
        (row ^ 1) * lax.axis_size("mp_1") + column,
    )
    first_own = (shard * copies + copy) * vocab
    first_other = (shard * copies + other_copy) * vocab
    place = jnp.stack([half, shard, quarter]).astype(jnp.int32)
    sizes = lax.axis_size("dp_0"), lax.axis_size("mp_0"), lax.axis_size("mp_1")
    pairs = pairs_of(sizes, lambda c, j, k: (j, k ^ 1) if c == 0 else (j ^ 1, k))
    beyond = pairs_of(
        sizes, lambda c, j, k: (j, beside(k, sizes[2])) if c == 0 else (beside(j, sizes[1]), k)
    )
    aslant = pairs_of(sizes, lambda c, j, k: (beside(j, sizes[1]), beside(k, sizes[2])))

    main, part_quarter = normalize(place, policy_hidden, reference_hidden, policy_gain, reference_gain)
    main, part_quarter, policy_send, reference_send = lax.optimization_barrier(
        (main, part_quarter, policy_embedding, reference_embedding)
    )
    main = lax.all_gather(main, DP, axis=0)
    policy_other = lax.ppermute(policy_send, DP_MP, pairs)
    reference_other = lax.ppermute(reference_send, DP_MP, pairs)
    held = lax.all_gather(part_quarter, DP, axis=0)
    opposite = lax.ppermute(held, DP_MP, aslant)
    fetched = lax.ppermute(held, DP_MP, beyond)
    swapped = lax.ppermute(fetched, "dp_1", [(0, 1), (1, 0)])
    quarters = [held, fetched, swapped, opposite]

    seqs = shards * part
    weights = mixture_weight.reshape(shards, 2, part)
    tokens = sampled_tokens.reshape(shards, 2, part)
    weight = lax.dynamic_index_in_dim(weights, half, 1, False).reshape(seqs, 1)
    token = lax.dynamic_index_in_dim(tokens, half, 1, False).reshape(seqs, 1)
    token = jnp.stack([token - first_own, token - first_other])
    weight = jnp.broadcast_to(weight, (seqs, 128))
    token = jnp.broadcast_to(token, (2, seqs, 128))
    weight_mine = lax.dynamic_slice_in_dim(mixture_weight, shard * seq_local, seq_local)[None]
    policy_other, reference_other, weight, token = lax.optimization_barrier(
        (policy_other, reference_other, weight, token)
    )
    diff_own, diff_send, block = mixture(
        place, main, quarters, policy_embedding, policy_other, reference_embedding, reference_other, weight, token
    )

    diff_other = lax.ppermute(diff_send, DP_MP, pairs)
    block = jnp.sum(lax.all_to_all(block, DP, 0, 0, tiled=True), axis=0, keepdims=True)
    block = jnp.broadcast_to(block, (copies,) + block.shape[1:])
    blocks = lax.all_to_all(block, MP, 0, 0, tiled=True)
    mixture_shift, sampled_logprobs = finish(
        place, lax.axis_size("mp_1"), diff_own, diff_other, blocks, weight_mine, shards
    )
    return (mixture_shift.reshape(shards * seq_local, vocab), sampled_logprobs)


def solution(mesh):
    split = Mesh(mesh.devices.reshape(8, 2, 8, 4), ("dp_0", "dp_1", "mp_0", "mp_1"))
    in_specs = (P(DP, None), P(DP, None), P(), P(), P(DP_MP, None), P(DP_MP, None), P(), P())
    out_specs = (P(None, DP_MP), P(None, DP))
    return jax.shard_map(local, mesh=split, in_specs=in_specs, out_specs=out_specs, check_vma=False)
```
